32 devices in a mesh: parts: 2 (over x), gx: 8 (over z, y), gy: 2 (over core).
Axes of the slice: x: 2, y: 2, z: 4, core: 2. Of those that a mesh axis runs over, the one named last changes fastest.
Arguments:
- field: float32 [2, 4096, 1024], P(None, ('parts', 'gx'), 'gy'), parts along dimension 1, may hold values from -6 to 6
- levels: int32 [4096, 1024], P(('parts', 'gx'), 'gy'), parts along dimension 0, may hold values from 0 to 255
- table: float32 [256], replicated, may hold values from 0 to 3
Outputs:
- near_field: float32 [2, 4096, 1024], P(None, ('parts', 'gx'), 'gy'), parts along dimension 1
- far_field: float32 [2048, 2, 1024], P(('parts', 'gx'), None, 'gy'), parts along dimension 0
The draws below stay inside these ranges and needn't reach their ends.
There are 2 independent parts, one for each index of `parts`. The reference program is written for one: setup_inputs(seed, part) draws one part's arguments, and reference() takes and returns one part's arrays. A program takes and returns all parts, laid end to end along the dimension named above; an argument that names none is the same for every part. Nothing has to cross between parts.
All inputs are finite; a program needn't handle non-finite values.
Results may differ from the reference program's by a relative error of at most 0.0003.
Values sent between devices are 32-bit elements; how exact they have to be, the bound alone decides.
A program may use at most 384 MiB of HBM per device.

```python
import math
import jax
import jax.numpy as jnp
from jax import lax

P_SIZE = 1024
Q = 1024
LEVELS = 256
STEPS = 8
NX = 2048
NY = 1024


def place_ends(array, stream_key, low, top_value):
    shape = array.shape
    spot = [jax.random.randint(jax.random.fold_in(stream_key, axis), (), 0, shape[axis]) for axis in range(len(shape))]
    array = array.at[tuple(spot)].set(low)
    longest = shape.index(max(shape))
    spot[longest] = (spot[longest] + 1) % shape[longest]
    return array.at[tuple(spot)].set(top_value)


def shard_levels(key, dims, pieces, low, largest):
    def one(axis_at, blocks):
        heights = jax.random.uniform(jax.random.fold_in(jax.random.fold_in(key, 6), axis_at), (blocks,), jnp.float32, low / len(pieces), largest / len(pieces))
        return jnp.repeat(jnp.exp(heights), dims[axis_at] // blocks).reshape((-1,) + (1,) * (len(dims) - axis_at - 1))

    level = one(*pieces[0])
    for cut in pieces[1:]:
        level = level * one(*cut)
    return level


def bell_draw(stream_key, dims, spread, most, pieces=(), kind=jnp.bfloat16):
    result = spread * jax.random.normal(stream_key, dims, jnp.float32)
    if pieces:
        result = result * shard_levels(stream_key, dims, pieces, -0.22, 0.18)
    return jnp.clip(result, -most, most).astype(kind)


def setup_inputs(seed: int = 0, part: int = 0) -> dict:
    splits = jax.random.split(jax.random.key(seed), 4)
    own_keys = jax.random.split(jax.random.fold_in(splits[3], part), 4)
    return {
        "field": bell_draw(own_keys[0], (2, NX, NY), 1.0, 6.0, ((1, 8), (2, 2)), jnp.float32),
        "levels": place_ends(jax.random.randint(own_keys[1], (NX, NY), 0, LEVELS), jax.random.fold_in(own_keys[1], 1), 0, LEVELS - 1).astype(jnp.int32),
        "table": jnp.clip(jax.random.uniform(splits[2], (LEVELS,), jnp.float32, 0.0, 3.0), 0.0, 3.0),
    }


def laplace(ext):
    centre = ext[:, 2:-2, 2:-2]
    near = ext[:, 1:-3, 2:-2] + ext[:, 3:-1, 2:-2] + ext[:, 2:-2, 1:-3] + ext[:, 2:-2, 3:-1]
    far = ext[:, :-4, 2:-2] + ext[:, 4:, 2:-2] + ext[:, 2:-2, :-4] + ext[:, 2:-2, 4:]
    return 4.0 / 3.0 * near - 1.0 / 12.0 * far - 5.0 * centre

def derivative(ext, contrast):
    lap = laplace(ext)
    centre = ext[:, 2:-2, 2:-2]
    real_part = lap[0] + contrast * centre[0]
    imag_part = lap[1] + contrast * centre[1]
    return jnp.stack([-imag_part, real_part])

def fourier(rows, cols, total, centre):
    phase = (rows[:, None] + total - centre) * cols[None, :] % total
    angle = 2.0 * math.pi / total * phase.astype(jnp.float32)
    scale = 1.0 / math.sqrt(total)
    return (jnp.cos(angle) * scale, jnp.sin(angle) * scale)

def padded(field):
    return jnp.pad(field, ((0, 0), (2, 2), (2, 2)))

def reference(field, levels, table):
    contrast = jnp.take(table, levels)
    state = field
    for step in range(STEPS):
        first = derivative(padded(state), contrast)
        middle = state + 0.075 * first
        second = derivative(padded(middle), contrast)
        state = state + 0.0375 * (first + second)
    near_re, near_im = (state[0], state[1])
    cos_x, sin_x = fourier(jnp.arange(P_SIZE).astype(jnp.int32), jnp.arange(NX).astype(jnp.int32), NX, P_SIZE // 2)
    hi = lax.Precision.HIGHEST
    part_re = jnp.dot(cos_x, near_re, precision=hi) + jnp.dot(sin_x, near_im, precision=hi)
    part_im = jnp.dot(cos_x, near_im, precision=hi) - jnp.dot(sin_x, near_re, precision=hi)
    cos_y, sin_y = fourier(jnp.arange(Q).astype(jnp.int32), jnp.arange(NY).astype(jnp.int32), NY, Q // 2)
    far_re = jnp.dot(part_re, cos_y.T, precision=hi) + jnp.dot(part_im, sin_y.T, precision=hi)
    far_im = jnp.dot(part_im, cos_y.T, precision=hi) - jnp.dot(part_re, sin_y.T, precision=hi)
    return (state, jnp.stack([far_re, far_im], axis=1))
```

```python
import functools
import math

import jax
import jax.numpy as jnp
from jax import lax
from jax.experimental import pallas as pl
from jax.experimental.pallas import tpu as pltpu
from jax.sharding import PartitionSpec as P

P_SIZE = 1024
Q = 1024
STEPS = 8
HALO = 4 * STEPS
LANES = 128
MESH = pl.DeviceIdType.MESH
F32 = jnp.float32
BF16 = jnp.bfloat16


def place(ix, iy):
    return (lax.axis_index("parts"), ix, iy)


def greet(neighbours):
    barrier = pltpu.get_barrier_semaphore()
    for device in neighbours:
        pl.semaphore_signal(barrier, inc=1, device_id=device, device_id_type=MESH)
    pl.semaphore_wait(barrier, len(neighbours))


def halo_kernel(count_x, field, levels, ext_f, ext_l, send, recv, own):
    rows, cols = levels.shape
    ix = lax.axis_index("gx")
    iy = lax.axis_index("gy")
    above = lax.rem(ix + count_x - 1, count_x)
    below = lax.rem(ix + 1, count_x)
    other = 1 - iy
    moves = (
        (place(ix, other), 0, rows, HALO, True),
        (place(above, iy), 0, HALO, HALO + rows, False),
        (place(below, iy), rows - HALO, HALO, 0, False),
        (place(above, other), 0, HALO, HALO + rows, True),
        (place(below, other), rows - HALO, HALO, 0, True),
    )
    greet([move[0] for move in moves])
    edge = pl.ds(pl.multiple_of((cols - LANES) * other, LANES), LANES)
    copies = []
    for k, (device, start, length, land, side) in enumerate(moves):
        src = pl.ds(start, length)
        dst = pl.ds(land, length)
        src_c = edge if side else pl.ds(0, cols)
        dst_c = pl.ds(cols, LANES) if side else pl.ds(0, cols)
        copies.append(
            pltpu.make_async_remote_copy(
                field.at[:, src, src_c], ext_f.at[:, dst, dst_c], send.at[2 * k], recv.at[2 * k],
                device_id=device, device_id_type=MESH,
            )
        )
        copies.append(
            pltpu.make_async_remote_copy(
                levels.at[src, src_c], ext_l.at[dst, dst_c], send.at[2 * k + 1], recv.at[2 * k + 1],
                device_id=device, device_id_type=MESH,
            )
        )
    for copy in copies:
        copy.start()
    inner = pl.ds(HALO, rows)
    mine = [
        pltpu.make_async_copy(field, ext_f.at[:, inner, pl.ds(0, cols)], own.at[0]),
        pltpu.make_async_copy(levels, ext_l.at[inner, pl.ds(0, cols)], own.at[1]),
    ]
    for copy in mine:
        copy.start()
    for copy in mine:
        copy.wait()
    for copy in copies:
        copy.wait()


def gather_halo(field, levels):
    _, rows, cols = field.shape
    tall, wide = (rows + 2 * HALO, cols + LANES)
    any_space = pl.BlockSpec(memory_space=pl.ANY)
    return pl.pallas_call(
        functools.partial(halo_kernel, lax.axis_size("gx")),
        out_shape=(
            jax.ShapeDtypeStruct((2, tall, wide), F32),
            jax.ShapeDtypeStruct((tall, wide), jnp.int32),
        ),
        in_specs=[any_space] * 2,
        out_specs=(any_space, any_space),
        scratch_shapes=[
            pltpu.SemaphoreType.DMA((10,)),
            pltpu.SemaphoreType.DMA((10,)),
            pltpu.SemaphoreType.DMA((2,)),
        ],
        compiler_params=pltpu.CompilerParams(collective_id=0, has_side_effects=True),
        name="halo",
    )(field, levels)


def heun_kernel(count_x, ext_f, ext_l, table, out, buf_f, buf_l, u, mid, con, weight, sem):
    blocks, tall, _ = buf_l.shape
    deep = tall // 8
    cols = (blocks - 1) * LANES
    rows = tall - 2 * HALO
    ix = lax.axis_index("gx")
    iy = lax.axis_index("gy")
    loads = []
    for j in range(blocks):
        lanes = pl.ds(j * LANES, LANES)
        loads.append(pltpu.make_async_copy(ext_l.at[:, lanes], buf_l.at[j], sem.at[0, j]))
        loads.append(pltpu.make_async_copy(ext_f.at[0, :, lanes], buf_f.at[0, j], sem.at[1, j]))
        loads.append(pltpu.make_async_copy(ext_f.at[1, :, lanes], buf_f.at[1, j], sem.at[2, j]))
    for copy in loads:
        copy.start()
    low = jnp.broadcast_to(table[0:1, :], (8, LANES))
    high = jnp.broadcast_to(table[1:2, :], (8, LANES))
    sub = lax.broadcasted_iota(jnp.int32, (8, LANES), 0)
    lane = lax.broadcasted_iota(jnp.int32, (8, LANES), 1)
    side = jnp.where((lane < LANES // 2) == (iy == 0), 1.0, 0.0).astype(F32)
    top = jnp.where(ix == 0, HALO, 0)
    bottom = jnp.where(ix == count_x - 1, HALO + rows, tall)
    for copy in loads:
        copy.wait()

    def prepare(r, carry):
        row = sub * deep + r
        inside = jnp.where((row >= top) & (row < bottom), 1.0, 0.0).astype(F32)
        for j in range(blocks):
            mask = inside * side if j == blocks - 1 else inside
            lanes = pl.ds(j * LANES, LANES)
            weight[r, :, lanes] = mask * (0.075 / 12.0)
            level = buf_l[j, pl.ds(r, 8, stride=deep), :]
            within = level & (LANES - 1)
            value = jnp.where(
                level < LANES,
                jnp.take_along_axis(low, within, axis=1),
                jnp.take_along_axis(high, within, axis=1),
            )
            con[r, :, lanes] = 12.0 * (value - 5.0)
            for c in range(2):
                u[c, r + 2, :, lanes] = mask * buf_f[c, j, pl.ds(r, 8, stride=deep), :]
        return carry

    lax.fori_loop(0, deep, prepare, 0)

    def wrap(ref):
        for c in range(2):
            for k in range(2):
                ref[c, k] = pltpu.roll(ref[c, deep + k], 1, 0)
                ref[c, deep + 2 + k] = pltpu.roll(ref[c, 2 + k], 7, 0)

    wide = blocks * LANES

    def twelve(ref, c, r):
        v = ref[c, r + 2]
        near = pltpu.roll(v, 1, 1) + pltpu.roll(v, wide - 1, 1) + (ref[c, r + 1] + ref[c, r + 3])
        far = pltpu.roll(v, 2, 1) + pltpu.roll(v, wide - 2, 1) + (ref[c, r] + ref[c, r + 4])
        return 16.0 * near - far + con[r] * v

    def step(_, carry):
        wrap(u)

        @pl.loop(0, deep, unroll=2)
        def _(r):
            w = weight[r]
            mid[0, r + 2] = u[0, r + 2] - w * twelve(u, 1, r)
            mid[1, r + 2] = u[1, r + 2] + w * twelve(u, 0, r)

        wrap(mid)

        @pl.loop(0, deep, unroll=2)
        def _(r):
            w = weight[r]
            u[0, r + 2] = 0.5 * ((u[0, r + 2] + mid[0, r + 2]) - w * twelve(mid, 1, r))
            u[1, r + 2] = 0.5 * ((u[1, r + 2] + mid[1, r + 2]) + w * twelve(mid, 0, r))

        return carry

    lax.fori_loop(0, STEPS, step, 0)

    def unpack(r, carry):
        for j in range(blocks - 1):
            for c in range(2):
                buf_f[c, j, pl.ds(r, 8, stride=deep), :] = u[c, r + 2, :, pl.ds(j * LANES, LANES)]
        return carry

    lax.fori_loop(0, deep, unpack, 0)
    for j in range(blocks - 1):
        for c in range(2):
            out[c, :, pl.ds(j * LANES, LANES)] = buf_f[c, j, pl.ds(HALO, rows), :]


def propagate(ext_f, ext_l, table):
    _, tall, wide = ext_f.shape
    blocks = wide // LANES
    deep = tall // 8
    any_space = pl.BlockSpec(memory_space=pl.ANY)
    vmem = pl.BlockSpec(memory_space=pltpu.VMEM)
    return pl.pallas_call(
        functools.partial(heun_kernel, lax.axis_size("gx")),
        out_shape=jax.ShapeDtypeStruct((2, tall - 2 * HALO, wide - LANES), F32),
        in_specs=[any_space, any_space, vmem],
        out_specs=vmem,
        scratch_shapes=[
            pltpu.VMEM((2, blocks, tall, LANES), F32),
            pltpu.VMEM((blocks, tall, LANES), jnp.int32),
            pltpu.VMEM((2, deep + 4, 8, wide), F32),
            pltpu.VMEM((2, deep + 4, 8, wide), F32),
            pltpu.VMEM((deep, 8, wide), F32),
            pltpu.VMEM((deep, 8, wide), F32),
            pltpu.SemaphoreType.DMA((3, blocks)),
        ],
        compiler_params=pltpu.CompilerParams(vmem_limit_bytes=40 * 1024 * 1024),
        name="heun",
    )(ext_f, ext_l, table.reshape(2, LANES))


def split(x):
    big = x.astype(BF16)
    return (big, (x - big.astype(F32)).astype(BF16))


def dot3(a, b):
    dot = functools.partial(jnp.dot, preferred_element_type=F32)
    return dot(a[0], b[0]) + (dot(a[0], b[1]) + dot(a[1], b[0]))


def far_kernel(
    near, e1c, e1s, e2c, e2s, yac, yas, ybc, ybs, out,
    raw, xc, xs, rhs, yc, ys, acc, from_up, from_dn, band, give, take,
    raw_send, raw_recv, up_send, up_recv, dn_send, dn_recv, side_send, side_recv,
):
    chunks, _, rows, _ = raw.shape
    groups = acc.shape[1]
    p_rows = acc.shape[2]
    half_q = yc.shape[3]
    ix = lax.axis_index("gx")
    iy = lax.axis_index("gy")
    z = ix // 2
    odd = lax.rem(ix, 2)
    count_x = 2 * groups
    pair = place(ix + 1 - 2 * odd, iy)
    higher = place(lax.rem(ix + 2, count_x), iy)
    lower = place(lax.rem(ix + count_x - 2, count_x), iy)
    side = place(ix, 1 - iy)
    greet([pair, higher, lower, side])

    def remote(src, dst, s, r, device):
        return pltpu.make_async_remote_copy(src, dst, s, r, device_id=device, device_id_type=MESH)

    raws = [
        remote(near.at[:, :, pl.ds(c * LANES, LANES)], raw.at[c], raw_send.at[c], raw_recv.at[c], pair)
        for c in range(chunks)
    ]
    for copy in raws:
        copy.start()

    for o in range(groups):
        a_c, a_s = (e1c[o : o + 1, :], e1s[o : o + 1, :])
        for k, part in enumerate(split(a_c * e2c[...] - a_s * e2s[...])):
            xc[k, pl.ds(o * p_rows, p_rows), :] = part
        for k, part in enumerate(split(a_s * e2c[...] + a_c * e2s[...])):
            xs[k, pl.ds(o * p_rows, p_rows), :] = part
    fine = ybc.shape[0]
    for h in range(2):
        q = pl.ds(h * half_q, half_q)
        for o in range(yac.shape[0]):
            a_c, a_s = (yac[o : o + 1, q], yas[o : o + 1, q])
            y = pl.ds(o * fine, fine)
            for k, part in enumerate(split(a_c * ybc[:, q] - a_s * ybs[:, q])):
                yc[h, k, y, :] = part
            for k, part in enumerate(split(a_s * ybc[:, q] + a_c * ybs[:, q])):
                ys[h, k, y, :] = part

    def up_copy(c, o):
        return remote(acc.at[c, o], from_up.at[c, o], up_send.at[c, o], up_recv.at[c, o], higher)

    def dn_copy(c, o):
        return remote(acc.at[c, o], from_dn.at[c, o], dn_send.at[c, o], dn_recv.at[c, o], lower)

    for c in range(chunks):
        raws[c].wait_recv()
        mine = pl.ds(pl.multiple_of(odd * rows, rows), rows)
        theirs = pl.ds(pl.multiple_of((1 - odd) * rows, rows), rows)
        for d in range(2):
            lanes = pl.ds(d * LANES, LANES)
            for k, part in enumerate(split(near[d, :, pl.ds(c * LANES, LANES)])):
                rhs[k, mine, lanes] = part
            for k, part in enumerate(split(raw[c, d])):
                rhs[k, theirs, lanes] = part
        right = (rhs[0], rhs[1])
        by_cos = dot3((xc[0], xc[1]), right)
        by_sin = dot3((xs[0], xs[1]), right)
        re = by_cos[:, :LANES] + by_sin[:, LANES:]
        im = by_cos[:, LANES:] - by_sin[:, :LANES]
        for o in range(groups):
            acc[c, o, :, pl.ds(0, LANES)] = re[o * p_rows : (o + 1) * p_rows]
            acc[c, o, :, pl.ds(LANES, LANES)] = im[o * p_rows : (o + 1) * p_rows]
        for k in range(groups):
            far_up, far_dn = (groups - 1 - k, k)

            @pl.when(z < far_up)
            def _():
                @pl.when(z > 0)
                def _():
                    up_copy(c, far_up).wait_recv()
                    acc[c, far_up] += from_up[c, far_up]

                up_copy(c, far_up).start()

            @pl.when(z > far_dn)
            def _():
                @pl.when(z < groups - 1)
                def _():
                    dn_copy(c, far_dn).wait_recv()
                    acc[c, far_dn] += from_dn[c, far_dn]

                dn_copy(c, far_dn).start()

    for c in range(chunks):
        for o in range(groups):

            @pl.when(z == o)
            def _():
                if o > 0:
                    up_copy(c, o).wait_recv()
                if o < groups - 1:
                    dn_copy(c, o).wait_recv()
                total = acc[c, o]
                if o > 0:
                    total = total + from_up[c, o]
                if o < groups - 1:
                    total = total + from_dn[c, o]
                for k, part in enumerate(split(total)):
                    band[k, pl.ds(0, p_rows), pl.ds(c * LANES, LANES)] = part[:, :LANES]
                    band[k, pl.ds(p_rows, p_rows), pl.ds(c * LANES, LANES)] = part[:, LANES:]

    left = (band[0], band[1])

    def angles(h):
        by_cos = dot3(left, (yc[h, 0], yc[h, 1]))
        by_sin = dot3(left, (ys[h, 0], ys[h, 1]))
        return (by_cos[:p_rows] + by_sin[p_rows:], by_cos[p_rows:] - by_sin[:p_rows])

    re, im = angles(1 - iy)
    give[0] = re
    give[1] = im
    swap = remote(give, take, side_send.at[0], side_recv.at[0], side)
    swap.start()
    re, im = angles(iy)
    swap.wait_recv()
    out[0] = re + take[0]
    out[1] = im + take[1]

    swap.wait_send()
    for copy in raws:
        copy.wait_send()
    for c in range(chunks):
        for o in range(groups):

            @pl.when(z < o)
            def _():
                up_copy(c, o).wait_send()

            @pl.when(z > o)
            def _():
                dn_copy(c, o).wait_send()


def turn(phase, total, scale):
    angle = 2.0 * math.pi / total * (phase % total).astype(F32)
    return (jnp.cos(angle) * scale, jnp.sin(angle) * scale)


def tables(rows, cols, count_x, count_y):
    index_x = lax.axis_index("gx")
    index_y = lax.axis_index("gy")
    total_x = rows * count_x
    total_y = cols * count_y
    p_rows = P_SIZE // count_x
    x = (index_x // 2) * 2 * rows + jnp.arange(2 * rows, dtype=jnp.int32)
    first = (2 * jnp.arange(count_x // 2, dtype=jnp.int32) + index_x % 2) * p_rows
    base = first + total_x - P_SIZE // 2
    e1 = turn(base[:, None] * x[None, :], total_x, 1.0 / math.sqrt(total_x))
    e2 = turn(jnp.arange(p_rows, dtype=jnp.int32)[:, None] * x[None, :], total_x, 1.0)
    fine = 32
    q = jnp.arange(Q, dtype=jnp.int32) + total_y - Q // 2
    coarse = index_y * cols + fine * jnp.arange(cols // fine, dtype=jnp.int32)
    ya = turn(coarse[:, None] * q[None, :], total_y, 1.0 / math.sqrt(total_y))
    yb = turn(jnp.arange(fine, dtype=jnp.int32)[:, None] * q[None, :], total_y, 1.0)
    return (*e1, *e2, *ya, *yb)


def far(near, angles, count_x):
    _, rows, cols = near.shape
    groups = count_x // 2
    p_rows = P_SIZE // count_x
    chunks = cols // LANES
    half_q = Q // 2
    vmem = pl.BlockSpec(memory_space=pltpu.VMEM)
    dma = pltpu.SemaphoreType.DMA
    stage = pltpu.VMEM((chunks, groups, p_rows, 2 * LANES), F32)
    return pl.pallas_call(
        far_kernel,
        out_shape=jax.ShapeDtypeStruct((2, p_rows, half_q), F32),
        in_specs=[vmem] * 9,
        out_specs=vmem,
        scratch_shapes=[
            pltpu.VMEM((chunks, 2, rows, LANES), F32),
            pltpu.VMEM((2, groups * p_rows, 2 * rows), BF16),
            pltpu.VMEM((2, groups * p_rows, 2 * rows), BF16),
            pltpu.VMEM((2, 2 * rows, 2 * LANES), BF16),
            pltpu.VMEM((2, 2, cols, half_q), BF16),
            pltpu.VMEM((2, 2, cols, half_q), BF16),
            stage,
            stage,
            stage,
            pltpu.VMEM((2, 2 * p_rows, cols), BF16),
            pltpu.VMEM((2, p_rows, half_q), F32),
            pltpu.VMEM((2, p_rows, half_q), F32),
            dma((chunks,)),
            dma((chunks,)),
            dma((chunks, groups)),
            dma((chunks, groups)),
            dma((chunks, groups)),
            dma((chunks, groups)),
            dma((1,)),
            dma((1,)),
        ],
        compiler_params=pltpu.CompilerParams(
            collective_id=1, has_side_effects=True, vmem_limit_bytes=48 * 1024 * 1024
        ),
        name="far",
    )(near, *angles)


def on_device(field, levels, table):
    _, rows, cols = field.shape
    count_x = lax.axis_size("gx")
    angles = tables(rows, cols, count_x, lax.axis_size("gy"))
    ext_f, ext_l = gather_halo(field, levels)
    near = propagate(ext_f, ext_l, table)
    return (near, jnp.transpose(far(near, angles, count_x), (1, 0, 2)))


def solution(mesh):
    in_specs = (P(None, ("parts", "gx"), "gy"), P(("parts", "gx"), "gy"), P())
    out_specs = (P(None, ("parts", "gx"), "gy"), P(("parts", "gx"), None, "gy"))
    return jax.shard_map(
        on_device, mesh=mesh, in_specs=in_specs, out_specs=out_specs, check_vma=False
    )
```

```python
import functools
import math

import jax
import jax.numpy as jnp
from jax import lax
from jax.experimental import pallas as pl
from jax.experimental.pallas import tpu as pltpu
from jax.sharding import PartitionSpec as P

P_SIZE = 1024
Q = 1024
STEPS = 8
HALO = 4 * STEPS
LANES = 128
MESH = pl.DeviceIdType.MESH
F32 = jnp.float32
BF16 = jnp.bfloat16


def place(ix, iy):
    return (lax.axis_index("parts"), ix, iy)


def greet(neighbours):
    barrier = pltpu.get_barrier_semaphore()
    for device in neighbours:
        pl.semaphore_signal(barrier, inc=1, device_id=device, device_id_type=MESH)
    pl.semaphore_wait(barrier, len(neighbours))


def halo_kernel(count_x, field, levels, ext_f, ext_l, send, recv):
    rows, cols = levels.shape
    ix = lax.axis_index("gx")
    iy = lax.axis_index("gy")
    above = lax.rem(ix + count_x - 1, count_x)
    below = lax.rem(ix + 1, count_x)
    other = 1 - iy
    moves = (
        (place(ix, other), 0, rows, HALO, True),
        (place(above, iy), 0, HALO, HALO + rows, False),
        (place(below, iy), rows - HALO, HALO, 0, False),
        (place(above, other), 0, HALO, HALO + rows, True),
        (place(below, other), rows - HALO, HALO, 0, True),
    )
    greet([move[0] for move in moves])
    edge = pl.ds(pl.multiple_of((cols - LANES) * other, LANES), LANES)
    copies = []
    for k, (device, start, length, land, side) in enumerate(moves):
        src = pl.ds(start, length)
        dst = pl.ds(land, length)
        src_c = edge if side else pl.ds(0, cols)
        dst_c = pl.ds(cols, LANES) if side else pl.ds(0, cols)
        copies.append(
            pltpu.make_async_remote_copy(
                field.at[:, src, src_c], ext_f.at[:, dst, dst_c], send.at[2 * k], recv.at[2 * k],
                device_id=device, device_id_type=MESH,
            )
        )
        copies.append(
            pltpu.make_async_remote_copy(
                levels.at[src, src_c], ext_l.at[dst, dst_c], send.at[2 * k + 1], recv.at[2 * k + 1],
                device_id=device, device_id_type=MESH,
            )
        )
    for copy in copies:
        copy.start()
    inner = pl.ds(HALO, rows)
    ext_f[:, inner, pl.ds(0, cols)] = field[...]
    ext_l[inner, pl.ds(0, cols)] = levels[...]
    for copy in copies:
        copy.wait()


def gather_halo(field, levels):
    _, rows, cols = field.shape
    tall, wide = (rows + 2 * HALO, cols + LANES)
    vmem = pl.BlockSpec(memory_space=pltpu.VMEM)
    return pl.pallas_call(
        functools.partial(halo_kernel, lax.axis_size("gx")),
        out_shape=(
            jax.ShapeDtypeStruct((2, tall, wide), F32),
            jax.ShapeDtypeStruct((tall, wide), jnp.int32),
        ),
        in_specs=[vmem] * 2,
        out_specs=(vmem, vmem),
        scratch_shapes=[
            pltpu.SemaphoreType.DMA((10,)),
            pltpu.SemaphoreType.DMA((10,)),
        ],
        compiler_params=pltpu.CompilerParams(collective_id=0, has_side_effects=True),
        name="halo",
    )(field, levels)


def shuffle(x, order):
    parts = [x.astype(BF16)]
    for _ in range(2):
        x = x - parts[-1].astype(F32)
        parts.append(x.astype(BF16))
    return sum(jnp.dot(part, order, preferred_element_type=F32) for part in parts)


def spread_order(shape, blocks, dim):
    spread = lax.broadcasted_iota(jnp.int32, shape, dim)
    plain = lax.broadcasted_iota(jnp.int32, shape, 1 - dim)
    return jnp.where(plain == (spread & (LANES - 1)) * blocks + spread // LANES, 1.0, 0.0).astype(BF16)


def heun_kernel(count_x, ext_f, ext_l, table, out, buf_f, buf_l, u, mid, con, weight):
    blocks, tall, _ = buf_l.shape
    deep = tall // 8
    wide = blocks * LANES
    cols = wide - LANES
    rows = tall - 2 * HALO
    ix = lax.axis_index("gx")
    iy = lax.axis_index("gy")
    order = spread_order((wide, wide), blocks, 1)
    for c in range(2):
        spread = shuffle(ext_f[c], order)
        for j in range(blocks):
            buf_f[c, j] = spread[:, j * LANES : (j + 1) * LANES]
    spread = jnp.dot(ext_l[...].astype(F32).astype(BF16), order, preferred_element_type=F32)
    for j in range(blocks):
        buf_l[j] = spread[:, j * LANES : (j + 1) * LANES].astype(jnp.int32)
    low = jnp.broadcast_to(table[0:1, :], (8, LANES))
    high = jnp.broadcast_to(table[1:2, :], (8, LANES))
    sub = lax.broadcasted_iota(jnp.int32, (8, LANES), 0)
    lane = lax.broadcasted_iota(jnp.int32, (8, LANES), 1)
    top = jnp.where(ix == 0, HALO, 0)
    bottom = jnp.where(ix == count_x - 1, HALO + rows, tall)
    middle = cols + LANES // 2
    sides = []
    for j in range(blocks):
        col = lane * blocks + j
        sides.append(jnp.where((col < cols) | ((col < middle) == (iy == 0)), 1.0, 0.0).astype(F32))

    def prepare(r, carry):
        row = sub * deep + r
        inside = jnp.where((row >= top) & (row < bottom), 1.0, 0.0).astype(F32)
        for j in range(blocks):
            mask = inside * sides[j]
            weight[j, r] = mask * (0.075 / 12.0)
            level = buf_l[j, pl.ds(r, 8, stride=deep), :]
            within = level & (LANES - 1)
            value = jnp.where(
                level < LANES,
                jnp.take_along_axis(low, within, axis=1),
                jnp.take_along_axis(high, within, axis=1),
            )
            con[j, r] = 12.0 * (value - 5.0)
            for c in range(2):
                u[c, j, r + 2] = mask * buf_f[c, j, pl.ds(r, 8, stride=deep), :]
        return carry

    lax.fori_loop(0, deep, prepare, 0)

    def wrap(ref):
        for c in range(2):
            for j in range(blocks):
                for k in range(2):
                    ref[c, j, k] = pltpu.roll(ref[c, j, deep + k], 1, 0)
                    ref[c, j, deep + 2 + k] = pltpu.roll(ref[c, j, 2 + k], 7, 0)

    tile = 4

    def twelve(ref, c, r):
        v = [[ref[c, j, r + k] for k in range(tile + 4)] for j in range(blocks)]
        line = {j: v[j][2 : tile + 2] for j in range(blocks)}
        for k in range(2):
            line[k - 2] = [pltpu.roll(x, 1, 1) for x in line[blocks + k - 2]]
            line[blocks + k] = [pltpu.roll(x, LANES - 1, 1) for x in line[k]]
        for j in range(blocks):
            for t in range(tile):
                near = (line[j - 1][t] + line[j + 1][t]) + (v[j][t + 1] + v[j][t + 3])
                far = (line[j - 2][t] + line[j + 2][t]) + (v[j][t] + v[j][t + 4])
                yield j, t, weight[j, r + t] * (16.0 * near - far + con[j, r + t] * v[j][t + 2])

    def step(_, carry):
        wrap(u)

        @pl.loop(0, deep // tile)
        def _(block):
            r = block * tile
            for j, t, k1 in twelve(u, 1, r):
                mid[0, j, r + t + 2] = u[0, j, r + t + 2] - k1
            for j, t, k1 in twelve(u, 0, r):
                mid[1, j, r + t + 2] = u[1, j, r + t + 2] + k1

        wrap(mid)

        @pl.loop(0, deep // tile)
        def _(block):
            r = block * tile
            for j, t, k2 in twelve(mid, 1, r):
                u[0, j, r + t + 2] = 0.5 * ((u[0, j, r + t + 2] + mid[0, j, r + t + 2]) - k2)
            for j, t, k2 in twelve(mid, 0, r):
                u[1, j, r + t + 2] = 0.5 * ((u[1, j, r + t + 2] + mid[1, j, r + t + 2]) + k2)

        return carry

    lax.fori_loop(0, STEPS, step, 0)

    def unpack(r, carry):
        for j in range(blocks):
            for c in range(2):
                buf_f[c, j, pl.ds(r, 8, stride=deep), :] = u[c, j, r + 2]
        return carry

    lax.fori_loop(0, deep, unpack, 0)
    order = spread_order((wide, cols), blocks, 0)
    for c in range(2):
        spread = jnp.concatenate([buf_f[c, j, pl.ds(HALO, rows), :] for j in range(blocks)], axis=1)
        out[c] = shuffle(spread, order)


def propagate(ext_f, ext_l, table):
    _, tall, wide = ext_f.shape
    blocks = wide // LANES
    deep = tall // 8
    vmem = pl.BlockSpec(memory_space=pltpu.VMEM)
    state = pltpu.VMEM((2, blocks, deep + 4, 8, LANES), F32)
    factor = pltpu.VMEM((blocks, deep, 8, LANES), F32)
    return pl.pallas_call(
        functools.partial(heun_kernel, lax.axis_size("gx")),
        out_shape=jax.ShapeDtypeStruct((2, tall - 2 * HALO, wide - LANES), F32),
        in_specs=[vmem, vmem, vmem],
        out_specs=vmem,
        scratch_shapes=[
            pltpu.VMEM((2, blocks, tall, LANES), F32),
            pltpu.VMEM((blocks, tall, LANES), jnp.int32),
            state,
            state,
            factor,
            factor,
        ],
        compiler_params=pltpu.CompilerParams(vmem_limit_bytes=40 * 1024 * 1024),
        name="heun",
    )(ext_f, ext_l, table.reshape(2, LANES))


def split(x):
    big = x.astype(BF16)
    return (big, (x - big.astype(F32)).astype(BF16))


def dot3(a, b):
    dot = functools.partial(jnp.dot, preferred_element_type=F32)
    return dot(a[0], b[0]) + (dot(a[0], b[1]) + dot(a[1], b[0]))


def far_kernel(
    near, e1c, e1s, e2c, e2s, yac, yas, ybc, ybs, out,
    raw, xc, xs, rhs, yc, ys, acc, from_up, from_dn, band, give, take,
    raw_send, raw_recv, up_send, up_recv, dn_send, dn_recv, side_send, side_recv,
):
    chunks, _, rows, _ = raw.shape
    groups = acc.shape[1]
    p_rows = acc.shape[2]
    half_q = yc.shape[3]
    ix = lax.axis_index("gx")
    iy = lax.axis_index("gy")
    z = ix // 2
    odd = lax.rem(ix, 2)
    count_x = 2 * groups
    pair = place(ix + 1 - 2 * odd, iy)
    higher = place(lax.rem(ix + 2, count_x), iy)
    lower = place(lax.rem(ix + count_x - 2, count_x), iy)
    side = place(ix, 1 - iy)
    greet([pair, higher, lower, side])

    def remote(src, dst, s, r, device):
        return pltpu.make_async_remote_copy(src, dst, s, r, device_id=device, device_id_type=MESH)

    raws = [
        remote(near.at[:, :, pl.ds(c * LANES, LANES)], raw.at[c], raw_send.at[c], raw_recv.at[c], pair)
        for c in range(chunks)
    ]
    for copy in raws:
        copy.start()

    for o in range(groups):
        a_c, a_s = (e1c[o : o + 1, :], e1s[o : o + 1, :])
        for k, part in enumerate(split(a_c * e2c[...] - a_s * e2s[...])):
            xc[k, pl.ds(o * p_rows, p_rows), :] = part
        for k, part in enumerate(split(a_s * e2c[...] + a_c * e2s[...])):
            xs[k, pl.ds(o * p_rows, p_rows), :] = part
    fine = ybc.shape[0]
    for h in range(2):
        q = pl.ds(h * half_q, half_q)
        for o in range(yac.shape[0]):
            a_c, a_s = (yac[o : o + 1, q], yas[o : o + 1, q])
            y = pl.ds(o * fine, fine)
            for k, part in enumerate(split(a_c * ybc[:, q] - a_s * ybs[:, q])):
                yc[h, k, y, :] = part
            for k, part in enumerate(split(a_s * ybc[:, q] + a_c * ybs[:, q])):
                ys[h, k, y, :] = part

    def up_copy(c, o):
        return remote(acc.at[c, o], from_up.at[c, o], up_send.at[c, o], up_recv.at[c, o], higher)

    def dn_copy(c, o):
        return remote(acc.at[c, o], from_dn.at[c, o], dn_send.at[c, o], dn_recv.at[c, o], lower)

    for c in range(chunks):
        raws[c].wait_recv()
        mine = pl.ds(pl.multiple_of(odd * rows, rows), rows)
        theirs = pl.ds(pl.multiple_of((1 - odd) * rows, rows), rows)
        for d in range(2):
            lanes = pl.ds(d * LANES, LANES)
            for k, part in enumerate(split(near[d, :, pl.ds(c * LANES, LANES)])):
                rhs[k, mine, lanes] = part
            for k, part in enumerate(split(raw[c, d])):
                rhs[k, theirs, lanes] = part
        right = (rhs[0], rhs[1])
        by_cos = dot3((xc[0], xc[1]), right)
        by_sin = dot3((xs[0], xs[1]), right)
        re = by_cos[:, :LANES] + by_sin[:, LANES:]
        im = by_cos[:, LANES:] - by_sin[:, :LANES]
        for o in range(groups):
            acc[c, o, :, pl.ds(0, LANES)] = re[o * p_rows : (o + 1) * p_rows]
            acc[c, o, :, pl.ds(LANES, LANES)] = im[o * p_rows : (o + 1) * p_rows]
        for k in range(groups):
            far_up, far_dn = (groups - 1 - k, k)

            @pl.when(z < far_up)
            def _():
                @pl.when(z > 0)
                def _():
                    up_copy(c, far_up).wait_recv()
                    acc[c, far_up] += from_up[c, far_up]

                up_copy(c, far_up).start()

            @pl.when(z > far_dn)
            def _():
                @pl.when(z < groups - 1)
                def _():
                    dn_copy(c, far_dn).wait_recv()
                    acc[c, far_dn] += from_dn[c, far_dn]

                dn_copy(c, far_dn).start()

    for c in range(chunks):
        for o in range(groups):

            @pl.when(z == o)
            def _():
                if o > 0:
                    up_copy(c, o).wait_recv()
                if o < groups - 1:
                    dn_copy(c, o).wait_recv()
                total = acc[c, o]
                if o > 0:
                    total = total + from_up[c, o]
                if o < groups - 1:
                    total = total + from_dn[c, o]
                for k, part in enumerate(split(total)):
                    band[k, pl.ds(0, p_rows), pl.ds(c * LANES, LANES)] = part[:, :LANES]
                    band[k, pl.ds(p_rows, p_rows), pl.ds(c * LANES, LANES)] = part[:, LANES:]

    left = (band[0], band[1])

    def angles(h):
        by_cos = dot3(left, (yc[h, 0], yc[h, 1]))
        by_sin = dot3(left, (ys[h, 0], ys[h, 1]))
        return (by_cos[:p_rows] + by_sin[p_rows:], by_cos[p_rows:] - by_sin[:p_rows])

    re, im = angles(1 - iy)
    give[0] = re
    give[1] = im
    swap = remote(give, take, side_send.at[0], side_recv.at[0], side)
    swap.start()
    re, im = angles(iy)
    swap.wait_recv()
    out[0] = re + take[0]
    out[1] = im + take[1]

    swap.wait_send()
    for copy in raws:
        copy.wait_send()
    for c in range(chunks):
        for o in range(groups):

            @pl.when(z < o)
            def _():
                up_copy(c, o).wait_send()

            @pl.when(z > o)
            def _():
                dn_copy(c, o).wait_send()


def turn(phase, total, scale):
    angle = 2.0 * math.pi / total * (phase % total).astype(F32)
    return (jnp.cos(angle) * scale, jnp.sin(angle) * scale)


def tables(rows, cols, count_x, count_y):
    index_x = lax.axis_index("gx")
    index_y = lax.axis_index("gy")
    total_x = rows * count_x
    total_y = cols * count_y
    p_rows = P_SIZE // count_x
    x = (index_x // 2) * 2 * rows + jnp.arange(2 * rows, dtype=jnp.int32)
    first = (2 * jnp.arange(count_x // 2, dtype=jnp.int32) + index_x % 2) * p_rows
    base = first + total_x - P_SIZE // 2
    e1 = turn(base[:, None] * x[None, :], total_x, 1.0 / math.sqrt(total_x))
    e2 = turn(jnp.arange(p_rows, dtype=jnp.int32)[:, None] * x[None, :], total_x, 1.0)
    fine = 32
    q = jnp.arange(Q, dtype=jnp.int32) + total_y - Q // 2
    coarse = index_y * cols + fine * jnp.arange(cols // fine, dtype=jnp.int32)
    ya = turn(coarse[:, None] * q[None, :], total_y, 1.0 / math.sqrt(total_y))
    yb = turn(jnp.arange(fine, dtype=jnp.int32)[:, None] * q[None, :], total_y, 1.0)
    return (*e1, *e2, *ya, *yb)


def far(near, angles, count_x):
    _, rows, cols = near.shape
    groups = count_x // 2
    p_rows = P_SIZE // count_x
    chunks = cols // LANES
    half_q = Q // 2
    vmem = pl.BlockSpec(memory_space=pltpu.VMEM)
    dma = pltpu.SemaphoreType.DMA
    stage = pltpu.VMEM((chunks, groups, p_rows, 2 * LANES), F32)
    return pl.pallas_call(
        far_kernel,
        out_shape=jax.ShapeDtypeStruct((2, p_rows, half_q), F32),
        in_specs=[vmem] * 9,
        out_specs=vmem,
        scratch_shapes=[
            pltpu.VMEM((chunks, 2, rows, LANES), F32),
            pltpu.VMEM((2, groups * p_rows, 2 * rows), BF16),
            pltpu.VMEM((2, groups * p_rows, 2 * rows), BF16),
            pltpu.VMEM((2, 2 * rows, 2 * LANES), BF16),
            pltpu.VMEM((2, 2, cols, half_q), BF16),
            pltpu.VMEM((2, 2, cols, half_q), BF16),
            stage,
            stage,
            stage,
            pltpu.VMEM((2, 2 * p_rows, cols), BF16),
            pltpu.VMEM((2, p_rows, half_q), F32),
            pltpu.VMEM((2, p_rows, half_q), F32),
            dma((chunks,)),
            dma((chunks,)),
            dma((chunks, groups)),
            dma((chunks, groups)),
            dma((chunks, groups)),
            dma((chunks, groups)),
            dma((1,)),
            dma((1,)),
        ],
        compiler_params=pltpu.CompilerParams(
            collective_id=1, has_side_effects=True, vmem_limit_bytes=48 * 1024 * 1024
        ),
        name="far",
    )(near, *angles)


def on_device(field, levels, table):
    _, rows, cols = field.shape
    count_x = lax.axis_size("gx")
    angles = tables(rows, cols, count_x, lax.axis_size("gy"))
    ext_f, ext_l = gather_halo(field, levels)
    near = propagate(ext_f, ext_l, table)
    return (near, jnp.transpose(far(near, angles, count_x), (1, 0, 2)))


def solution(mesh):
    in_specs = (P(None, ("parts", "gx"), "gy"), P(("parts", "gx"), "gy"), P())
    out_specs = (P(None, ("parts", "gx"), "gy"), P(("parts", "gx"), None, "gy"))
    return jax.shard_map(
        on_device, mesh=mesh, in_specs=in_specs, out_specs=out_specs, check_vma=False
    )
```

```python
import functools
import math

import jax
import jax.numpy as jnp
from jax import lax
from jax.experimental import pallas as pl
from jax.experimental.pallas import tpu as pltpu
from jax.sharding import PartitionSpec as P

P_SIZE = 1024
Q = 1024
STEPS = 8
HALO = 4 * STEPS
LANES = 128
MESH = pl.DeviceIdType.MESH
F32 = jnp.float32
BF16 = jnp.bfloat16


def place(ix, iy):
    return (lax.axis_index("parts"), ix, iy)


def greet(neighbours):
    barrier = pltpu.get_barrier_semaphore()
    for device in neighbours:
        pl.semaphore_signal(barrier, inc=1, device_id=device, device_id_type=MESH)
    pl.semaphore_wait(barrier, len(neighbours))


def halo_kernel(count_x, field, levels, rows_f, rows_l, side_f, side_l, send, recv):
    rows, cols = levels.shape
    ix = lax.axis_index("gx")
    iy = lax.axis_index("gy")
    above = lax.rem(ix + count_x - 1, count_x)
    below = lax.rem(ix + 1, count_x)
    other = 1 - iy
    greet([place(ix, other), place(above, iy), place(below, iy), place(above, other), place(below, other)])
    edge = pl.ds(pl.multiple_of((cols - LANES) * other, LANES), LANES)
    all_c = pl.ds(0, cols)
    out_c = pl.ds(cols, LANES)
    first = pl.ds(0, HALO)
    last = pl.ds(rows - HALO, HALO)
    whole = pl.ds(0, rows)

    def move(k, device, src, src_c, dst_f, dst_l):
        pairs = ((field.at[:, src, src_c], dst_f), (levels.at[src, src_c], dst_l))
        return [
            pltpu.make_async_remote_copy(
                a, b, send.at[2 * k + i], recv.at[2 * k + i], device_id=device, device_id_type=MESH
            )
            for i, (a, b) in enumerate(pairs)
        ]

    def land(end, lanes):
        return (rows_f.at[end, :, :, lanes], rows_l.at[end, :, lanes])

    upward = move(1, place(above, iy), first, all_c, *land(1, all_c))
    upward += move(3, place(above, other), first, edge, *land(1, out_c))
    downward = move(2, place(below, iy), last, all_c, *land(0, all_c))
    downward += move(4, place(below, other), last, edge, *land(0, out_c))
    across = move(0, place(ix, other), whole, edge, side_f, side_l)

    @pl.when(ix > 0)
    def _():
        for copy in upward:
            copy.start()

    @pl.when(ix < count_x - 1)
    def _():
        for copy in downward:
            copy.start()

    for copy in across:
        copy.start()

    @pl.when(ix == 0)
    def _():
        rows_f[0] = jnp.zeros_like(rows_f[0])
        rows_l[0] = jnp.zeros_like(rows_l[0])

    @pl.when(ix == count_x - 1)
    def _():
        rows_f[1] = jnp.zeros_like(rows_f[1])
        rows_l[1] = jnp.zeros_like(rows_l[1])

    for copy in across:
        copy.wait()

    @pl.when(ix > 0)
    def _():
        for copy in downward:
            copy.wait_recv()
        for copy in upward:
            copy.wait_send()

    @pl.when(ix < count_x - 1)
    def _():
        for copy in upward:
            copy.wait_recv()
        for copy in downward:
            copy.wait_send()


def gather_halo(field, levels):
    _, rows, cols = field.shape
    wide = cols + LANES
    vmem = pl.BlockSpec(memory_space=pltpu.VMEM)
    return pl.pallas_call(
        functools.partial(halo_kernel, lax.axis_size("gx")),
        out_shape=(
            jax.ShapeDtypeStruct((2, 2, HALO, wide), F32),
            jax.ShapeDtypeStruct((2, HALO, wide), jnp.int32),
            jax.ShapeDtypeStruct((2, rows, LANES), F32),
            jax.ShapeDtypeStruct((rows, LANES), jnp.int32),
        ),
        in_specs=[vmem] * 2,
        out_specs=(vmem,) * 4,
        scratch_shapes=[pltpu.SemaphoreType.DMA((10,)), pltpu.SemaphoreType.DMA((10,))],
        compiler_params=pltpu.CompilerParams(collective_id=0, has_side_effects=True),
        name="halo",
    )(field, levels)


def shuffle(x, order):
    parts = [x.astype(BF16)]
    for _ in range(2):
        x = x - parts[-1].astype(F32)
        parts.append(x.astype(BF16))
    return sum(jnp.dot(part, order, preferred_element_type=F32) for part in parts)


def spread_order(shape, blocks, dim):
    spread = lax.broadcasted_iota(jnp.int32, shape, dim)
    plain = lax.broadcasted_iota(jnp.int32, shape, 1 - dim)
    return jnp.where(plain == (spread & (LANES - 1)) * blocks + spread // LANES, 1.0, 0.0).astype(BF16)


def heun_kernel(
    count_x, field, levels, rows_f, rows_l, side_f, side_l, table, out, buf_f, buf_l, u, mid, con, weight
):
    blocks, tall, _ = buf_l.shape
    deep = tall // 8
    wide = blocks * LANES
    cols = wide - LANES
    rows = tall - 2 * HALO
    ix = lax.axis_index("gx")
    iy = lax.axis_index("gy")
    order = spread_order((wide, wide), blocks, 1)
    pieces = ((0, HALO), (HALO, rows), (HALO + rows, HALO))
    for c in range(2):
        body = jnp.concatenate([field[c], side_f[c]], axis=1)
        for (start, length), part in zip(pieces, (rows_f[0, c], body, rows_f[1, c])):
            spread = shuffle(part, order)
            for j in range(blocks):
                buf_f[c, j, pl.ds(start, length), :] = spread[:, j * LANES : (j + 1) * LANES]
    body = jnp.concatenate([levels[...], side_l[...]], axis=1)
    for (start, length), part in zip(pieces, (rows_l[0], body, rows_l[1])):
        spread = jnp.dot(part.astype(F32).astype(BF16), order, preferred_element_type=F32)
        for j in range(blocks):
            buf_l[j, pl.ds(start, length), :] = spread[:, j * LANES : (j + 1) * LANES].astype(jnp.int32)
    low = jnp.broadcast_to(table[0:1, :], (8, LANES))
    high = jnp.broadcast_to(table[1:2, :], (8, LANES))
    sub = lax.broadcasted_iota(jnp.int32, (8, LANES), 0)
    lane = lax.broadcasted_iota(jnp.int32, (8, LANES), 1)
    top = jnp.where(ix == 0, HALO, 0)
    bottom = jnp.where(ix == count_x - 1, HALO + rows, tall)
    middle = cols + LANES // 2
    sides = []
    for j in range(blocks):
        col = lane * blocks + j
        sides.append(jnp.where((col < cols) | ((col < middle) == (iy == 0)), 1.0, 0.0).astype(F32))

    def prepare(r, carry):
        row = sub * deep + r
        inside = jnp.where((row >= top) & (row < bottom), 1.0, 0.0).astype(F32)
        for j in range(blocks):
            mask = inside * sides[j]
            weight[j, r] = mask * (0.075 / 12.0)
            level = buf_l[j, pl.ds(r, 8, stride=deep), :]
            within = level & (LANES - 1)
            value = jnp.where(
                level < LANES,
                jnp.take_along_axis(low, within, axis=1),
                jnp.take_along_axis(high, within, axis=1),
            )
            con[j, r] = 12.0 * (value - 5.0)
            for c in range(2):
                u[c, j, r + 2] = mask * buf_f[c, j, pl.ds(r, 8, stride=deep), :]
        return carry

    lax.fori_loop(0, deep, prepare, 0)

    def wrap(ref):
        for c in range(2):
            for j in range(blocks):
                for k in range(2):
                    ref[c, j, k] = pltpu.roll(ref[c, j, deep + k], 1, 0)
                    ref[c, j, deep + 2 + k] = pltpu.roll(ref[c, j, 2 + k], 7, 0)

    tile = 4

    def twelve(ref, c, r):
        v = [[ref[c, j, r + k] for k in range(tile + 4)] for j in range(blocks)]
        line = {j: v[j][2 : tile + 2] for j in range(blocks)}
        for k in range(2):
            line[k - 2] = [pltpu.roll(x, 1, 1) for x in line[blocks + k - 2]]
            line[blocks + k] = [pltpu.roll(x, LANES - 1, 1) for x in line[k]]
        for j in range(blocks):
            for t in range(tile):
                near = (line[j - 1][t] + line[j + 1][t]) + (v[j][t + 1] + v[j][t + 3])
                far = (line[j - 2][t] + line[j + 2][t]) + (v[j][t] + v[j][t + 4])
                yield j, t, weight[j, r + t] * (16.0 * near - far + con[j, r + t] * v[j][t + 2])

    def step(_, carry):
        wrap(u)

        @pl.loop(0, deep // tile)
        def _(block):
            r = block * tile
            for j, t, k1 in twelve(u, 1, r):
                mid[0, j, r + t + 2] = u[0, j, r + t + 2] - k1
            for j, t, k1 in twelve(u, 0, r):
                mid[1, j, r + t + 2] = u[1, j, r + t + 2] + k1

        wrap(mid)

        @pl.loop(0, deep // tile)
        def _(block):
            r = block * tile
            for j, t, k2 in twelve(mid, 1, r):
                u[0, j, r + t + 2] = 0.5 * ((u[0, j, r + t + 2] + mid[0, j, r + t + 2]) - k2)
            for j, t, k2 in twelve(mid, 0, r):
                u[1, j, r + t + 2] = 0.5 * ((u[1, j, r + t + 2] + mid[1, j, r + t + 2]) + k2)

        return carry

    lax.fori_loop(0, STEPS, step, 0)

    def unpack(r, carry):
        for j in range(blocks):
            for c in range(2):
                buf_f[c, j, pl.ds(r, 8, stride=deep), :] = u[c, j, r + 2]
        return carry

    lax.fori_loop(0, deep, unpack, 0)
    order = spread_order((wide, cols), blocks, 0)
    for c in range(2):
        spread = jnp.concatenate([buf_f[c, j, pl.ds(HALO, rows), :] for j in range(blocks)], axis=1)
        out[c] = shuffle(spread, order)


def propagate(field, levels, halo, table):
    _, rows, cols = field.shape
    tall = rows + 2 * HALO
    blocks = cols // LANES + 1
    deep = tall // 8
    vmem = pl.BlockSpec(memory_space=pltpu.VMEM)
    state = pltpu.VMEM((2, blocks, deep + 4, 8, LANES), F32)
    factor = pltpu.VMEM((blocks, deep, 8, LANES), F32)
    return pl.pallas_call(
        functools.partial(heun_kernel, lax.axis_size("gx")),
        out_shape=jax.ShapeDtypeStruct((2, rows, cols), F32),
        in_specs=[vmem] * 7,
        out_specs=vmem,
        scratch_shapes=[
            pltpu.VMEM((2, blocks, tall, LANES), F32),
            pltpu.VMEM((blocks, tall, LANES), jnp.int32),
            state,
            state,
            factor,
            factor,
        ],
        compiler_params=pltpu.CompilerParams(vmem_limit_bytes=40 * 1024 * 1024),
        name="heun",
    )(field, levels, *halo, table.reshape(2, LANES))


def split(x):
    big = x.astype(BF16)
    return (big, (x - big.astype(F32)).astype(BF16))


def dot3(a, b):
    dot = functools.partial(jnp.dot, preferred_element_type=F32)
    return dot(a[0], b[0]) + (dot(a[0], b[1]) + dot(a[1], b[0]))


def far_kernel(
    near, e1c, e1s, e2c, e2s, yac, yas, ybc, ybs, out,
    raw, xc, xs, rhs, yc, ys, acc, from_up, from_dn, band, far, give, take,
    raw_send, raw_recv, up_send, up_recv, dn_send, dn_recv, side_send, side_recv,
):
    chunks, _, rows, _ = raw.shape
    groups = acc.shape[1]
    p_rows = acc.shape[2]
    half_q = yc.shape[3]
    ix = lax.axis_index("gx")
    iy = lax.axis_index("gy")
    z = ix // 2
    odd = lax.rem(ix, 2)
    count_x = 2 * groups
    pair = place(ix + 1 - 2 * odd, iy)
    higher = place(lax.rem(ix + 2, count_x), iy)
    lower = place(lax.rem(ix + count_x - 2, count_x), iy)
    side = place(ix, 1 - iy)
    greet([pair, higher, lower, side])

    def remote(src, dst, s, r, device):
        return pltpu.make_async_remote_copy(src, dst, s, r, device_id=device, device_id_type=MESH)

    raws = [
        remote(near.at[:, :, pl.ds(c * LANES, LANES)], raw.at[c], raw_send.at[c], raw_recv.at[c], pair)
        for c in range(chunks)
    ]
    for copy in raws:
        copy.start()

    for o in range(groups):
        a_c, a_s = (e1c[o : o + 1, :], e1s[o : o + 1, :])
        for k, part in enumerate(split(a_c * e2c[...] - a_s * e2s[...])):
            xc[k, pl.ds(o * p_rows, p_rows), :] = part
        for k, part in enumerate(split(a_s * e2c[...] + a_c * e2s[...])):
            xs[k, pl.ds(o * p_rows, p_rows), :] = part
    fine = ybc.shape[0]
    for h in range(2):
        q = pl.ds(h * half_q, half_q)
        for o in range(yac.shape[0]):
            a_c, a_s = (yac[o : o + 1, q], yas[o : o + 1, q])
            y = pl.ds(o * fine, fine)
            for k, part in enumerate(split(a_c * ybc[:, q] - a_s * ybs[:, q])):
                yc[h, k, y, :] = part
            for k, part in enumerate(split(a_s * ybc[:, q] + a_c * ybs[:, q])):
                ys[h, k, y, :] = part

    def up_copy(c, o):
        return remote(acc.at[c, o], from_up.at[c, o], up_send.at[c, o], up_recv.at[c, o], higher)

    def dn_copy(c, o):
        return remote(acc.at[c, o], from_dn.at[c, o], dn_send.at[c, o], dn_recv.at[c, o], lower)

    def transform(c):
        raws[c].wait_recv()
        mine = pl.ds(pl.multiple_of(odd * rows, rows), rows)
        theirs = pl.ds(pl.multiple_of((1 - odd) * rows, rows), rows)
        for d in range(2):
            lanes = pl.ds(d * LANES, LANES)
            for k, part in enumerate(split(near[d, :, pl.ds(c * LANES, LANES)])):
                rhs[k, mine, lanes] = part
            for k, part in enumerate(split(raw[c, d])):
                rhs[k, theirs, lanes] = part
        right = (rhs[0], rhs[1])
        by_cos = dot3((xc[0], xc[1]), right)
        by_sin = dot3((xs[0], xs[1]), right)
        re = by_cos[:, :LANES] + by_sin[:, LANES:]
        im = by_cos[:, LANES:] - by_sin[:, :LANES]
        for o in range(groups):
            acc[c, o, :, pl.ds(0, LANES)] = re[o * p_rows : (o + 1) * p_rows]
            acc[c, o, :, pl.ds(LANES, LANES)] = im[o * p_rows : (o + 1) * p_rows]

    def originate(c):
        @pl.when(z == 0)
        def _():
            for o in reversed(range(1, groups)):
                up_copy(c, o).start()

        @pl.when(z == groups - 1)
        def _():
            for o in range(groups - 1):
                dn_copy(c, o).start()

    def forward(c):
        for k in range(groups):
            far_up, far_dn = (groups - 1 - k, k)

            @pl.when((z > 0) & (z < far_up))
            def _():
                up_copy(c, far_up).wait_recv()
                acc[c, far_up] += from_up[c, far_up]
                up_copy(c, far_up).start()

            @pl.when((z < groups - 1) & (z > far_dn))
            def _():
                dn_copy(c, far_dn).wait_recv()
                acc[c, far_dn] += from_dn[c, far_dn]
                dn_copy(c, far_dn).start()

    def collect(g):
        for o in range(groups):

            @pl.when(z == o)
            def _():
                for i in range(2):
                    c = 2 * g + i
                    total = acc[c, o]
                    if o > 0:
                        up_copy(c, o).wait_recv()
                        total = total + from_up[c, o]
                    if o < groups - 1:
                        dn_copy(c, o).wait_recv()
                        total = total + from_dn[c, o]
                    for k, part in enumerate(split(total)):
                        band[g, k, pl.ds(0, p_rows), pl.ds(i * LANES, LANES)] = part[:, :LANES]
                        band[g, k, pl.ds(p_rows, p_rows), pl.ds(i * LANES, LANES)] = part[:, LANES:]

    def angles(g, h):
        left = (band[g, 0], band[g, 1])
        y = pl.ds(2 * g * LANES, 2 * LANES)
        by_cos = dot3(left, (yc[h, 0, y], yc[h, 1, y]))
        by_sin = dot3(left, (ys[h, 0, y], ys[h, 1, y]))
        return (by_cos[:p_rows] + by_sin[p_rows:], by_cos[p_rows:] - by_sin[:p_rows])

    final = chunks // 2 - 1

    def accumulate(g):
        for h in range(2):
            for d, value in enumerate(angles(g, h)):
                far[h, d] = value if g == 0 else far[h, d] + value

    for c in range(chunks):
        transform(c)
        originate(c)
        if c > 0:
            forward(c - 1)
        if c >= 3 and c % 2 == 1:
            collect(c // 2 - 1)
            accumulate(c // 2 - 1)
    forward(chunks - 1)
    collect(final)

    def finish(h):
        pair_of = angles(final, h)
        return [far[h, d] + pair_of[d] for d in range(2)]

    give[0], give[1] = finish(1 - iy)
    swap = remote(give, take, side_send.at[0], side_recv.at[0], side)
    swap.start()
    re, im = finish(iy)
    swap.wait_recv()
    out[0] = re + take[0]
    out[1] = im + take[1]

    swap.wait_send()
    for copy in raws:
        copy.wait_send()
    for c in range(chunks):
        for o in range(groups):

            @pl.when(z < o)
            def _():
                up_copy(c, o).wait_send()

            @pl.when(z > o)
            def _():
                dn_copy(c, o).wait_send()


def turn(phase, total, scale):
    angle = 2.0 * math.pi / total * (phase % total).astype(F32)
    return (jnp.cos(angle) * scale, jnp.sin(angle) * scale)


def tables(rows, cols, count_x, count_y):
    index_x = lax.axis_index("gx")
    index_y = lax.axis_index("gy")
    total_x = rows * count_x
    total_y = cols * count_y
    p_rows = P_SIZE // count_x
    x = (index_x // 2) * 2 * rows + jnp.arange(2 * rows, dtype=jnp.int32)
    first = (2 * jnp.arange(count_x // 2, dtype=jnp.int32) + index_x % 2) * p_rows
    base = first + total_x - P_SIZE // 2
    e1 = turn(base[:, None] * x[None, :], total_x, 1.0 / math.sqrt(total_x))
    e2 = turn(jnp.arange(p_rows, dtype=jnp.int32)[:, None] * x[None, :], total_x, 1.0)
    fine = 32
    q = jnp.arange(Q, dtype=jnp.int32) + total_y - Q // 2
    coarse = index_y * cols + fine * jnp.arange(cols // fine, dtype=jnp.int32)
    ya = turn(coarse[:, None] * q[None, :], total_y, 1.0 / math.sqrt(total_y))
    yb = turn(jnp.arange(fine, dtype=jnp.int32)[:, None] * q[None, :], total_y, 1.0)
    return (*e1, *e2, *ya, *yb)


def far(near, angles, count_x):
    _, rows, cols = near.shape
    groups = count_x // 2
    p_rows = P_SIZE // count_x
    chunks = cols // LANES
    half_q = Q // 2
    vmem = pl.BlockSpec(memory_space=pltpu.VMEM)
    dma = pltpu.SemaphoreType.DMA
    stage = pltpu.VMEM((chunks, groups, p_rows, 2 * LANES), F32)
    return pl.pallas_call(
        far_kernel,
        out_shape=jax.ShapeDtypeStruct((2, p_rows, half_q), F32),
        in_specs=[vmem] * 9,
        out_specs=vmem,
        scratch_shapes=[
            pltpu.VMEM((chunks, 2, rows, LANES), F32),
            pltpu.VMEM((2, groups * p_rows, 2 * rows), BF16),
            pltpu.VMEM((2, groups * p_rows, 2 * rows), BF16),
            pltpu.VMEM((2, 2 * rows, 2 * LANES), BF16),
            pltpu.VMEM((2, 2, cols, half_q), BF16),
            pltpu.VMEM((2, 2, cols, half_q), BF16),
            stage,
            stage,
            stage,
            pltpu.VMEM((chunks // 2, 2, 2 * p_rows, 2 * LANES), BF16),
            pltpu.VMEM((2, 2, p_rows, half_q), F32),
            pltpu.VMEM((2, p_rows, half_q), F32),
            pltpu.VMEM((2, p_rows, half_q), F32),
            dma((chunks,)),
            dma((chunks,)),
            dma((chunks, groups)),
            dma((chunks, groups)),
            dma((chunks, groups)),
            dma((chunks, groups)),
            dma((1,)),
            dma((1,)),
        ],
        compiler_params=pltpu.CompilerParams(
            collective_id=1, has_side_effects=True, vmem_limit_bytes=48 * 1024 * 1024
        ),
        name="far",
    )(near, *angles)


def on_device(field, levels, table):
    _, rows, cols = field.shape
    count_x = lax.axis_size("gx")
    angles = tables(rows, cols, count_x, lax.axis_size("gy"))
    near = propagate(field, levels, gather_halo(field, levels), table)
    return (near, jnp.transpose(far(near, angles, count_x), (1, 0, 2)))


def solution(mesh):
    in_specs = (P(None, ("parts", "gx"), "gy"), P(("parts", "gx"), "gy"), P())
    out_specs = (P(None, ("parts", "gx"), "gy"), P(("parts", "gx"), None, "gy"))
    return jax.shard_map(
        on_device, mesh=mesh, in_specs=in_specs, out_specs=out_specs, check_vma=False
    )
```

```python
import functools
import math

import jax
import jax.numpy as jnp
from jax import lax
from jax.experimental import pallas as pl
from jax.experimental.pallas import tpu as pltpu
from jax.sharding import PartitionSpec as P

P_SIZE = 1024
Q = 1024
STEPS = 8
HALO = 4 * STEPS
LANES = 128
MESH = pl.DeviceIdType.MESH
F32 = jnp.float32
BF16 = jnp.bfloat16


def place(ix, iy):
    return (lax.axis_index("parts"), ix, iy)


def greet(neighbours):
    barrier = pltpu.get_barrier_semaphore()
    for device in neighbours:
        pl.semaphore_signal(barrier, inc=1, device_id=device, device_id_type=MESH)
    pl.semaphore_wait(barrier, len(neighbours))


def halo_kernel(count_x, field, levels, rows_f, rows_l, side_f, side_l, send, recv):
    rows, cols = levels.shape
    ix = lax.axis_index("gx")
    iy = lax.axis_index("gy")
    above = lax.rem(ix + count_x - 1, count_x)
    below = lax.rem(ix + 1, count_x)
    other = 1 - iy
    greet([place(ix, other), place(above, iy), place(below, iy), place(above, other), place(below, other)])
    edge = pl.ds(pl.multiple_of((cols - LANES) * other, LANES), LANES)
    all_c = pl.ds(0, cols)
    out_c = pl.ds(cols, LANES)
    first = pl.ds(0, HALO)
    last = pl.ds(rows - HALO, HALO)
    whole = pl.ds(0, rows)

    def move(k, device, src, src_c, dst_f, dst_l):
        pairs = ((field.at[:, src, src_c], dst_f), (levels.at[src, src_c], dst_l))
        return [
            pltpu.make_async_remote_copy(
                a, b, send.at[2 * k + i], recv.at[2 * k + i], device_id=device, device_id_type=MESH
            )
            for i, (a, b) in enumerate(pairs)
        ]

    def land(end, lanes):
        return (rows_f.at[end, :, :, lanes], rows_l.at[end, :, lanes])

    upward = move(1, place(above, iy), first, all_c, *land(1, all_c))
    upward += move(3, place(above, other), first, edge, *land(1, out_c))
    downward = move(2, place(below, iy), last, all_c, *land(0, all_c))
    downward += move(4, place(below, other), last, edge, *land(0, out_c))
    across = move(0, place(ix, other), whole, edge, side_f, side_l)

    @pl.when(ix > 0)
    def _():
        for copy in upward:
            copy.start()

    @pl.when(ix < count_x - 1)
    def _():
        for copy in downward:
            copy.start()

    for copy in across:
        copy.start()

    @pl.when(ix == 0)
    def _():
        rows_f[0] = jnp.zeros_like(rows_f[0])
        rows_l[0] = jnp.zeros_like(rows_l[0])

    @pl.when(ix == count_x - 1)
    def _():
        rows_f[1] = jnp.zeros_like(rows_f[1])
        rows_l[1] = jnp.zeros_like(rows_l[1])

    for copy in across:
        copy.wait()

    @pl.when(ix > 0)
    def _():
        for copy in downward:
            copy.wait_recv()
        for copy in upward:
            copy.wait_send()

    @pl.when(ix < count_x - 1)
    def _():
        for copy in upward:
            copy.wait_recv()
        for copy in downward:
            copy.wait_send()


def gather_halo(field, levels):
    _, rows, cols = field.shape
    wide = cols + LANES
    vmem = pl.BlockSpec(memory_space=pltpu.VMEM)
    return pl.pallas_call(
        functools.partial(halo_kernel, lax.axis_size("gx")),
        out_shape=(
            jax.ShapeDtypeStruct((2, 2, HALO, wide), F32),
            jax.ShapeDtypeStruct((2, HALO, wide), jnp.int32),
            jax.ShapeDtypeStruct((2, rows, LANES), F32),
            jax.ShapeDtypeStruct((rows, LANES), jnp.int32),
        ),
        in_specs=[vmem] * 2,
        out_specs=(vmem,) * 4,
        scratch_shapes=[pltpu.SemaphoreType.DMA((10,)), pltpu.SemaphoreType.DMA((10,))],
        compiler_params=pltpu.CompilerParams(collective_id=0, has_side_effects=True),
        name="halo",
    )(field, levels)


def shuffle(x, order):
    parts = [x.astype(BF16)]
    for _ in range(2):
        x = x - parts[-1].astype(F32)
        parts.append(x.astype(BF16))
    return sum(jnp.dot(part, order, preferred_element_type=F32) for part in parts)


def spread_order(shape, blocks, dim):
    spread = lax.broadcasted_iota(jnp.int32, shape, dim)
    plain = lax.broadcasted_iota(jnp.int32, shape, 1 - dim)
    return jnp.where(plain == (spread & (LANES - 1)) * blocks + spread // LANES, 1.0, 0.0).astype(BF16)


def heun_kernel(
    count_x, field, levels, far_rows_f, far_rows_l, far_side_f, far_side_l, table, out,
    rows_f, rows_l, side_f, side_l, sem, buf_f, buf_l, u, mid, con, weight
):
    blocks, tall, _ = buf_l.shape
    deep = tall // 8
    wide = blocks * LANES
    cols = wide - LANES
    rows = tall - 2 * HALO
    ix = lax.axis_index("gx")
    iy = lax.axis_index("gy")
    loads = [
        pltpu.make_async_copy(far_side_l, side_l, sem.at[0]),
        pltpu.make_async_copy(far_side_f, side_f, sem.at[1]),
        pltpu.make_async_copy(far_rows_l, rows_l, sem.at[2]),
        pltpu.make_async_copy(far_rows_f, rows_f, sem.at[3]),
    ]
    for copy in loads:
        copy.start()
    order = spread_order((wide, wide), blocks, 1)

    def keep_f(part, c, start, length):
        spread = shuffle(part, order)
        for j in range(blocks):
            buf_f[c, j, pl.ds(start, length), :] = spread[:, j * LANES : (j + 1) * LANES]

    def keep_l(part, start, length):
        spread = jnp.dot(part.astype(F32).astype(BF16), order, preferred_element_type=F32)
        for j in range(blocks):
            buf_l[j, pl.ds(start, length), :] = spread[:, j * LANES : (j + 1) * LANES].astype(jnp.int32)

    loads[0].wait()
    keep_l(jnp.concatenate([levels[...], side_l[...]], axis=1), HALO, rows)
    loads[1].wait()
    for c in range(2):
        keep_f(jnp.concatenate([field[c], side_f[c]], axis=1), c, HALO, rows)
    loads[2].wait()
    loads[3].wait()
    for end, start in ((0, 0), (1, HALO + rows)):
        keep_l(rows_l[end], start, HALO)
        for c in range(2):
            keep_f(rows_f[end, c], c, start, HALO)
    low = jnp.broadcast_to(table[0:1, :], (8, LANES))
    high = jnp.broadcast_to(table[1:2, :], (8, LANES))
    sub = lax.broadcasted_iota(jnp.int32, (8, LANES), 0)
    lane = lax.broadcasted_iota(jnp.int32, (8, LANES), 1)
    top = jnp.where(ix == 0, HALO, 0)
    bottom = jnp.where(ix == count_x - 1, HALO + rows, tall)
    middle = cols + LANES // 2
    sides = []
    for j in range(blocks):
        col = lane * blocks + j
        sides.append(jnp.where((col < cols) | ((col < middle) == (iy == 0)), 1.0, 0.0).astype(F32))

    def prepare(r, carry):
        row = sub * deep + r
        inside = jnp.where((row >= top) & (row < bottom), 1.0, 0.0).astype(F32)
        for j in range(blocks):
            mask = inside * sides[j]
            weight[j, r] = mask * (0.075 / 12.0)
            level = buf_l[j, pl.ds(r, 8, stride=deep), :]
            within = level & (LANES - 1)
            value = jnp.where(
                level < LANES,
                jnp.take_along_axis(low, within, axis=1),
                jnp.take_along_axis(high, within, axis=1),
            )
            con[j, r] = 12.0 * (value - 5.0)
            for c in range(2):
                u[c, j, r + 2] = mask * buf_f[c, j, pl.ds(r, 8, stride=deep), :]
        return carry

    lax.fori_loop(0, deep, prepare, 0)

    def wrap(ref):
        for c in range(2):
            for j in range(blocks):
                for k in range(2):
                    ref[c, j, k] = pltpu.roll(ref[c, j, deep + k], 1, 0)
                    ref[c, j, deep + 2 + k] = pltpu.roll(ref[c, j, 2 + k], 7, 0)

    tile = 4

    def twelve(ref, c, r):
        v = [[ref[c, j, r + k] for k in range(tile + 4)] for j in range(blocks)]
        line = {j: v[j][2 : tile + 2] for j in range(blocks)}
        for k in range(2):
            line[k - 2] = [pltpu.roll(x, 1, 1) for x in line[blocks + k - 2]]
            line[blocks + k] = [pltpu.roll(x, LANES - 1, 1) for x in line[k]]
        for j in range(blocks):
            for t in range(tile):
                near = (line[j - 1][t] + line[j + 1][t]) + (v[j][t + 1] + v[j][t + 3])
                far = (line[j - 2][t] + line[j + 2][t]) + (v[j][t] + v[j][t + 4])
                yield j, t, weight[j, r + t] * (16.0 * near - far + con[j, r + t] * v[j][t + 2])

    def step(_, carry):
        wrap(u)

        @pl.loop(0, deep // tile)
        def _(block):
            r = block * tile
            for j, t, k1 in twelve(u, 1, r):
                mid[0, j, r + t + 2] = u[0, j, r + t + 2] - k1
            for j, t, k1 in twelve(u, 0, r):
                mid[1, j, r + t + 2] = u[1, j, r + t + 2] + k1

        wrap(mid)

        @pl.loop(0, deep // tile)
        def _(block):
            r = block * tile
            for j, t, k2 in twelve(mid, 1, r):
                u[0, j, r + t + 2] = 0.5 * ((u[0, j, r + t + 2] + mid[0, j, r + t + 2]) - k2)
            for j, t, k2 in twelve(mid, 0, r):
                u[1, j, r + t + 2] = 0.5 * ((u[1, j, r + t + 2] + mid[1, j, r + t + 2]) + k2)

        return carry

    lax.fori_loop(0, STEPS, step, 0)

    def unpack(r, carry):
        for j in range(blocks):
            for c in range(2):
                buf_f[c, j, pl.ds(r, 8, stride=deep), :] = u[c, j, r + 2]
        return carry

    lax.fori_loop(0, deep, unpack, 0)
    order = spread_order((wide, cols), blocks, 0)
    for c in range(2):
        spread = jnp.concatenate([buf_f[c, j, pl.ds(HALO, rows), :] for j in range(blocks)], axis=1)
        out[c] = shuffle(spread, order)


def propagate(field, levels, halo, table):
    _, rows, cols = field.shape
    tall = rows + 2 * HALO
    blocks = cols // LANES + 1
    wide = blocks * LANES
    deep = tall // 8
    vmem = pl.BlockSpec(memory_space=pltpu.VMEM)
    state = pltpu.VMEM((2, blocks, deep + 4, 8, LANES), F32)
    factor = pltpu.VMEM((blocks, deep, 8, LANES), F32)
    return pl.pallas_call(
        functools.partial(heun_kernel, lax.axis_size("gx")),
        out_shape=jax.ShapeDtypeStruct((2, rows, cols), F32),
        in_specs=[vmem] * 2 + [pl.BlockSpec(memory_space=pl.ANY)] * 4 + [vmem],
        out_specs=vmem,
        scratch_shapes=[
            pltpu.VMEM((2, 2, HALO, wide), F32),
            pltpu.VMEM((2, HALO, wide), jnp.int32),
            pltpu.VMEM((2, rows, LANES), F32),
            pltpu.VMEM((rows, LANES), jnp.int32),
            pltpu.SemaphoreType.DMA((4,)),
            pltpu.VMEM((2, blocks, tall, LANES), F32),
            pltpu.VMEM((blocks, tall, LANES), jnp.int32),
            state,
            state,
            factor,
            factor,
        ],
        compiler_params=pltpu.CompilerParams(vmem_limit_bytes=40 * 1024 * 1024),
        name="heun",
    )(field, levels, *halo, table.reshape(2, LANES))


def split(x):
    big = x.astype(BF16)
    return (big, (x - big.astype(F32)).astype(BF16))


def dot3(a, b):
    dot = functools.partial(jnp.dot, preferred_element_type=F32)
    return dot(a[0], b[0]) + (dot(a[0], b[1]) + dot(a[1], b[0]))


def far_kernel(
    near, e1c, e1s, e2c, e2s, yac, yas, ybc, ybs, out,
    raw, xc, xs, rhs, yc, ys, acc, from_up, from_dn, band, far, give, take,
    raw_send, raw_recv, up_send, up_recv, dn_send, dn_recv, side_send, side_recv,
):
    chunks, _, rows, _ = raw.shape
    groups = acc.shape[1]
    p_rows = acc.shape[2]
    half_q = yc.shape[3]
    ix = lax.axis_index("gx")
    iy = lax.axis_index("gy")
    z = ix // 2
    odd = lax.rem(ix, 2)
    count_x = 2 * groups
    pair = place(ix + 1 - 2 * odd, iy)
    higher = place(lax.rem(ix + 2, count_x), iy)
    lower = place(lax.rem(ix + count_x - 2, count_x), iy)
    side = place(ix, 1 - iy)
    greet([pair, higher, lower, side])

    def remote(src, dst, s, r, device):
        return pltpu.make_async_remote_copy(src, dst, s, r, device_id=device, device_id_type=MESH)

    raws = [
        remote(near.at[:, :, pl.ds(c * LANES, LANES)], raw.at[c], raw_send.at[c], raw_recv.at[c], pair)
        for c in range(chunks)
    ]
    for copy in raws:
        copy.start()

    for o in range(groups):
        a_c, a_s = (e1c[o : o + 1, :], e1s[o : o + 1, :])
        for k, part in enumerate(split(a_c * e2c[...] - a_s * e2s[...])):
            xc[k, pl.ds(o * p_rows, p_rows), :] = part
        for k, part in enumerate(split(a_s * e2c[...] + a_c * e2s[...])):
            xs[k, pl.ds(o * p_rows, p_rows), :] = part
    fine = ybc.shape[0]
    for h in range(2):
        q = pl.ds(h * half_q, half_q)
        for o in range(yac.shape[0]):
            a_c, a_s = (yac[o : o + 1, q], yas[o : o + 1, q])
            y = pl.ds(o * fine, fine)
            for k, part in enumerate(split(a_c * ybc[:, q] - a_s * ybs[:, q])):
                yc[h, k, y, :] = part
            for k, part in enumerate(split(a_s * ybc[:, q] + a_c * ybs[:, q])):
                ys[h, k, y, :] = part

    def up_copy(c, o):
        return remote(acc.at[c, o], from_up.at[c, o], up_send.at[c, o], up_recv.at[c, o], higher)

    def dn_copy(c, o):
        return remote(acc.at[c, o], from_dn.at[c, o], dn_send.at[c, o], dn_recv.at[c, o], lower)

    def transform(c):
        raws[c].wait_recv()
        mine = pl.ds(pl.multiple_of(odd * rows, rows), rows)
        theirs = pl.ds(pl.multiple_of((1 - odd) * rows, rows), rows)
        for d in range(2):
            lanes = pl.ds(d * LANES, LANES)
            for k, part in enumerate(split(near[d, :, pl.ds(c * LANES, LANES)])):
                rhs[k, mine, lanes] = part
            for k, part in enumerate(split(raw[c, d])):
                rhs[k, theirs, lanes] = part
        right = (rhs[0], rhs[1])
        by_cos = dot3((xc[0], xc[1]), right)
        by_sin = dot3((xs[0], xs[1]), right)
        re = by_cos[:, :LANES] + by_sin[:, LANES:]
        im = by_cos[:, LANES:] - by_sin[:, :LANES]
        for o in range(groups):
            acc[c, o, :, pl.ds(0, LANES)] = re[o * p_rows : (o + 1) * p_rows]
            acc[c, o, :, pl.ds(LANES, LANES)] = im[o * p_rows : (o + 1) * p_rows]

    def originate(c):
        @pl.when(z == 0)
        def _():
            for o in reversed(range(1, groups)):
                up_copy(c, o).start()

        @pl.when(z == groups - 1)
        def _():
            for o in range(groups - 1):
                dn_copy(c, o).start()

    def forward(c):
        for k in range(groups):
            far_up, far_dn = (groups - 1 - k, k)

            @pl.when((z > 0) & (z < far_up))
            def _():
                up_copy(c, far_up).wait_recv()
                acc[c, far_up] += from_up[c, far_up]
                up_copy(c, far_up).start()

            @pl.when((z < groups - 1) & (z > far_dn))
            def _():
                dn_copy(c, far_dn).wait_recv()
                acc[c, far_dn] += from_dn[c, far_dn]
                dn_copy(c, far_dn).start()

    def collect(g):
        for o in range(groups):

            @pl.when(z == o)
            def _():
                for i in range(2):
                    c = 2 * g + i
                    total = acc[c, o]
                    if o > 0:
                        up_copy(c, o).wait_recv()
                        total = total + from_up[c, o]
                    if o < groups - 1:
                        dn_copy(c, o).wait_recv()
                        total = total + from_dn[c, o]
                    for k, part in enumerate(split(total)):
                        band[g, k, pl.ds(0, p_rows), pl.ds(i * LANES, LANES)] = part[:, :LANES]
                        band[g, k, pl.ds(p_rows, p_rows), pl.ds(i * LANES, LANES)] = part[:, LANES:]

    def angles(g, h):
        left = (band[g, 0], band[g, 1])
        y = pl.ds(2 * g * LANES, 2 * LANES)
        by_cos = dot3(left, (yc[h, 0, y], yc[h, 1, y]))
        by_sin = dot3(left, (ys[h, 0, y], ys[h, 1, y]))
        return (by_cos[:p_rows] + by_sin[p_rows:], by_cos[p_rows:] - by_sin[:p_rows])

    final = chunks // 2 - 1

    def accumulate(g):
        for h in range(2):
            for d, value in enumerate(angles(g, h)):
                far[h, d] = value if g == 0 else far[h, d] + value

    for c in range(chunks):
        transform(c)
        originate(c)
        if c > 0:
            forward(c - 1)
        if c >= 3 and c % 2 == 1:
            collect(c // 2 - 1)
            accumulate(c // 2 - 1)
    forward(chunks - 1)
    collect(final)

    def finish(h):
        pair_of = angles(final, h)
        return [far[h, d] + pair_of[d] for d in range(2)]

    give[0], give[1] = finish(1 - iy)
    swap = remote(give, take, side_send.at[0], side_recv.at[0], side)
    swap.start()
    re, im = finish(iy)
    swap.wait_recv()
    out[0] = re + take[0]
    out[1] = im + take[1]

    swap.wait_send()
    for copy in raws:
        copy.wait_send()
    for c in range(chunks):
        for o in range(groups):

            @pl.when(z < o)
            def _():
                up_copy(c, o).wait_send()

            @pl.when(z > o)
            def _():
                dn_copy(c, o).wait_send()


def turn(phase, total, scale):
    angle = 2.0 * math.pi / total * (phase % total).astype(F32)
    return (jnp.cos(angle) * scale, jnp.sin(angle) * scale)


def tables(rows, cols, count_x, count_y):
    index_x = lax.axis_index("gx")
    index_y = lax.axis_index("gy")
    total_x = rows * count_x
    total_y = cols * count_y
    p_rows = P_SIZE // count_x
    x = (index_x // 2) * 2 * rows + jnp.arange(2 * rows, dtype=jnp.int32)
    first = (2 * jnp.arange(count_x // 2, dtype=jnp.int32) + index_x % 2) * p_rows
    base = first + total_x - P_SIZE // 2
    e1 = turn(base[:, None] * x[None, :], total_x, 1.0 / math.sqrt(total_x))
    e2 = turn(jnp.arange(p_rows, dtype=jnp.int32)[:, None] * x[None, :], total_x, 1.0)
    fine = 32
    q = jnp.arange(Q, dtype=jnp.int32) + total_y - Q // 2
    coarse = index_y * cols + fine * jnp.arange(cols // fine, dtype=jnp.int32)
    ya = turn(coarse[:, None] * q[None, :], total_y, 1.0 / math.sqrt(total_y))
    yb = turn(jnp.arange(fine, dtype=jnp.int32)[:, None] * q[None, :], total_y, 1.0)
    return (*e1, *e2, *ya, *yb)


def far(near, angles, count_x):
    _, rows, cols = near.shape
    groups = count_x // 2
    p_rows = P_SIZE // count_x
    chunks = cols // LANES
    half_q = Q // 2
    vmem = pl.BlockSpec(memory_space=pltpu.VMEM)
    dma = pltpu.SemaphoreType.DMA
    stage = pltpu.VMEM((chunks, groups, p_rows, 2 * LANES), F32)
    return pl.pallas_call(
        far_kernel,
        out_shape=jax.ShapeDtypeStruct((2, p_rows, half_q), F32),
        in_specs=[vmem] * 9,
        out_specs=vmem,
        scratch_shapes=[
            pltpu.VMEM((chunks, 2, rows, LANES), F32),
            pltpu.VMEM((2, groups * p_rows, 2 * rows), BF16),
            pltpu.VMEM((2, groups * p_rows, 2 * rows), BF16),
            pltpu.VMEM((2, 2 * rows, 2 * LANES), BF16),
            pltpu.VMEM((2, 2, cols, half_q), BF16),
            pltpu.VMEM((2, 2, cols, half_q), BF16),
            stage,
            stage,
            stage,
            pltpu.VMEM((chunks // 2, 2, 2 * p_rows, 2 * LANES), BF16),
            pltpu.VMEM((2, 2, p_rows, half_q), F32),
            pltpu.VMEM((2, p_rows, half_q), F32),
            pltpu.VMEM((2, p_rows, half_q), F32),
            dma((chunks,)),
            dma((chunks,)),
            dma((chunks, groups)),
            dma((chunks, groups)),
            dma((chunks, groups)),
            dma((chunks, groups)),
            dma((1,)),
            dma((1,)),
        ],
        compiler_params=pltpu.CompilerParams(
            collective_id=1, has_side_effects=True, vmem_limit_bytes=48 * 1024 * 1024
        ),
        name="far",
    )(near, *angles)


def on_device(field, levels, table):
    _, rows, cols = field.shape
    count_x = lax.axis_size("gx")
    angles = tables(rows, cols, count_x, lax.axis_size("gy"))
    near = propagate(field, levels, gather_halo(field, levels), table)
    return (near, jnp.transpose(far(near, angles, count_x), (1, 0, 2)))


def solution(mesh):
    in_specs = (P(None, ("parts", "gx"), "gy"), P(("parts", "gx"), "gy"), P())
    out_specs = (P(None, ("parts", "gx"), "gy"), P(("parts", "gx"), None, "gy"))
    return jax.shard_map(
        on_device, mesh=mesh, in_specs=in_specs, out_specs=out_specs, check_vma=False
    )
```

```python
import functools
import math

import jax
import jax.numpy as jnp
from jax import lax
from jax.experimental import pallas as pl
from jax.experimental.pallas import tpu as pltpu
from jax.sharding import PartitionSpec as P

P_SIZE = 1024
Q = 1024
STEPS = 8
HALO = 4 * STEPS
LANES = 128
MESH = pl.DeviceIdType.MESH
F32 = jnp.float32
BF16 = jnp.bfloat16


def place(ix, iy):
    return (lax.axis_index("parts"), ix, iy)


def greet(neighbours):
    barrier = pltpu.get_barrier_semaphore()
    for device in neighbours:
        pl.semaphore_signal(barrier, inc=1, device_id=device, device_id_type=MESH)
    pl.semaphore_wait(barrier, len(neighbours))


def halo_kernel(count_x, field, levels, rows_f, rows_l, side_f, side_l, send, recv):
    rows, cols = levels.shape
    ix = lax.axis_index("gx")
    iy = lax.axis_index("gy")
    above = lax.rem(ix + count_x - 1, count_x)
    below = lax.rem(ix + 1, count_x)
    other = 1 - iy
    greet([place(ix, other), place(above, iy), place(below, iy), place(above, other), place(below, other)])
    edge = pl.ds(pl.multiple_of((cols - LANES) * other, LANES), LANES)
    all_c = pl.ds(0, cols)
    out_c = pl.ds(cols, LANES)
    first = pl.ds(0, HALO)
    last = pl.ds(rows - HALO, HALO)
    whole = pl.ds(0, rows)

    def move(k, device, src, src_c, dst_f, dst_l):
        pairs = ((field.at[:, src, src_c], dst_f), (levels.at[src, src_c], dst_l))
        return [
            pltpu.make_async_remote_copy(
                a, b, send.at[2 * k + i], recv.at[2 * k + i], device_id=device, device_id_type=MESH
            )
            for i, (a, b) in enumerate(pairs)
        ]

    def land(end, lanes):
        return (rows_f.at[end, :, :, lanes], rows_l.at[end, :, lanes])

    upward = move(1, place(above, iy), first, all_c, *land(1, all_c))
    upward += move(3, place(above, other), first, edge, *land(1, out_c))
    downward = move(2, place(below, iy), last, all_c, *land(0, all_c))
    downward += move(4, place(below, other), last, edge, *land(0, out_c))
    across = move(0, place(ix, other), whole, edge, side_f, side_l)

    @pl.when(ix > 0)
    def _():
        for copy in upward:
            copy.start()

    @pl.when(ix < count_x - 1)
    def _():
        for copy in downward:
            copy.start()

    for copy in across:
        copy.start()

    @pl.when(ix == 0)
    def _():
        rows_f[0] = jnp.zeros_like(rows_f[0])
        rows_l[0] = jnp.zeros_like(rows_l[0])

    @pl.when(ix == count_x - 1)
    def _():
        rows_f[1] = jnp.zeros_like(rows_f[1])
        rows_l[1] = jnp.zeros_like(rows_l[1])

    for copy in across:
        copy.wait()

    @pl.when(ix > 0)
    def _():
        for copy in downward:
            copy.wait_recv()
        for copy in upward:
            copy.wait_send()

    @pl.when(ix < count_x - 1)
    def _():
        for copy in upward:
            copy.wait_recv()
        for copy in downward:
            copy.wait_send()


def gather_halo(field, levels):
    _, rows, cols = field.shape
    wide = cols + LANES
    vmem = pl.BlockSpec(memory_space=pltpu.VMEM)
    return pl.pallas_call(
        functools.partial(halo_kernel, lax.axis_size("gx")),
        out_shape=(
            jax.ShapeDtypeStruct((2, 2, HALO, wide), F32),
            jax.ShapeDtypeStruct((2, HALO, wide), jnp.int32),
            jax.ShapeDtypeStruct((2, rows, LANES), F32),
            jax.ShapeDtypeStruct((rows, LANES), jnp.int32),
        ),
        in_specs=[vmem] * 2,
        out_specs=(vmem,) * 4,
        scratch_shapes=[pltpu.SemaphoreType.DMA((10,)), pltpu.SemaphoreType.DMA((10,))],
        compiler_params=pltpu.CompilerParams(collective_id=0, has_side_effects=True),
        name="halo",
    )(field, levels)


def shuffle(x, order):
    parts = [x.astype(BF16)]
    for _ in range(2):
        x = x - parts[-1].astype(F32)
        parts.append(x.astype(BF16))
    return sum(jnp.dot(part, order, preferred_element_type=F32) for part in parts)


def spread_order(shape, blocks, dim):
    spread = lax.broadcasted_iota(jnp.int32, shape, dim)
    plain = lax.broadcasted_iota(jnp.int32, shape, 1 - dim)
    return jnp.where(plain == (spread & (LANES - 1)) * blocks + spread // LANES, 1.0, 0.0).astype(BF16)


def heun_kernel(
    count_x, field, levels, far_rows_f, far_rows_l, far_side_f, far_side_l, table, out,
    rows_f, rows_l, side_f, side_l, sem, buf_f, buf_l, u, mid, con, weight
):
    blocks, tall, _ = buf_l.shape
    deep = tall // 8
    wide = blocks * LANES
    cols = wide - LANES
    rows = tall - 2 * HALO
    ix = lax.axis_index("gx")
    iy = lax.axis_index("gy")
    loads = [
        pltpu.make_async_copy(far_side_l, side_l, sem.at[0]),
        pltpu.make_async_copy(far_side_f, side_f, sem.at[1]),
        pltpu.make_async_copy(far_rows_l, rows_l, sem.at[2]),
        pltpu.make_async_copy(far_rows_f, rows_f, sem.at[3]),
    ]
    for copy in loads:
        copy.start()
    order = spread_order((wide, wide), blocks, 1)

    def keep_f(part, c, start, length):
        spread = shuffle(part, order)
        for j in range(blocks):
            buf_f[c, j, pl.ds(start, length), :] = spread[:, j * LANES : (j + 1) * LANES]

    def keep_l(part, start, length):
        spread = jnp.dot(part.astype(F32).astype(BF16), order, preferred_element_type=F32)
        for j in range(blocks):
            buf_l[j, pl.ds(start, length), :] = spread[:, j * LANES : (j + 1) * LANES].astype(jnp.int32)

    loads[0].wait()
    keep_l(jnp.concatenate([levels[...], side_l[...]], axis=1), HALO, rows)
    loads[1].wait()
    for c in range(2):
        keep_f(jnp.concatenate([field[c], side_f[c]], axis=1), c, HALO, rows)
    loads[2].wait()
    loads[3].wait()
    for end, start in ((0, 0), (1, HALO + rows)):
        keep_l(rows_l[end], start, HALO)
        for c in range(2):
            keep_f(rows_f[end, c], c, start, HALO)
    low = jnp.broadcast_to(table[0:1, :], (8, LANES))
    high = jnp.broadcast_to(table[1:2, :], (8, LANES))
    sub = lax.broadcasted_iota(jnp.int32, (8, LANES), 0)
    lane = lax.broadcasted_iota(jnp.int32, (8, LANES), 1)
    top = jnp.where(ix == 0, HALO, 0)
    bottom = jnp.where(ix == count_x - 1, HALO + rows, tall)
    middle = cols + LANES // 2
    sides = []
    for j in range(blocks):
        col = lane * blocks + j
        sides.append(jnp.where((col < cols) | ((col < middle) == (iy == 0)), 1.0, 0.0).astype(F32))

    def prepare(r, carry):
        row = sub * deep + r
        inside = jnp.where((row >= top) & (row < bottom), 1.0, 0.0).astype(F32)
        for j in range(blocks):
            mask = inside * sides[j]
            weight[j, r] = mask * (0.075 / 12.0)
            level = buf_l[j, pl.ds(r, 8, stride=deep), :]
            within = level & (LANES - 1)
            value = jnp.where(
                level < LANES,
                jnp.take_along_axis(low, within, axis=1),
                jnp.take_along_axis(high, within, axis=1),
            )
            con[j, r] = 12.0 * (value - 5.0)
            for c in range(2):
                u[c, j, r + 2] = mask * buf_f[c, j, pl.ds(r, 8, stride=deep), :]
        return carry

    lax.fori_loop(0, deep, prepare, 0)

    def wrap(ref):
        for c in range(2):
            for j in range(blocks):
                for k in range(2):
                    ref[c, j, k] = pltpu.roll(ref[c, j, deep + k], 1, 0)
                    ref[c, j, deep + 2 + k] = pltpu.roll(ref[c, j, 2 + k], 7, 0)

    tile = 4

    def twelve(ref, c, r):
        v = [[ref[c, j, r + k] for k in range(tile + 4)] for j in range(blocks)]
        line = {j: v[j][2 : tile + 2] for j in range(blocks)}
        for k in range(2):
            line[k - 2] = [pltpu.roll(x, 1, 1) for x in line[blocks + k - 2]]
            line[blocks + k] = [pltpu.roll(x, LANES - 1, 1) for x in line[k]]
        for j in range(blocks):
            for t in range(tile):
                near = (line[j - 1][t] + line[j + 1][t]) + (v[j][t + 1] + v[j][t + 3])
                far = (line[j - 2][t] + line[j + 2][t]) + (v[j][t] + v[j][t + 4])
                yield j, t, weight[j, r + t] * (16.0 * near - far + con[j, r + t] * v[j][t + 2])

    def step(_, carry):
        wrap(u)

        @pl.loop(0, deep // tile)
        def _(block):
            r = block * tile
            for j, t, k1 in twelve(u, 1, r):
                mid[0, j, r + t + 2] = u[0, j, r + t + 2] - k1
            for j, t, k1 in twelve(u, 0, r):
                mid[1, j, r + t + 2] = u[1, j, r + t + 2] + k1

        wrap(mid)

        @pl.loop(0, deep // tile)
        def _(block):
            r = block * tile
            for j, t, k2 in twelve(mid, 1, r):
                u[0, j, r + t + 2] = 0.5 * ((u[0, j, r + t + 2] + mid[0, j, r + t + 2]) - k2)
            for j, t, k2 in twelve(mid, 0, r):
                u[1, j, r + t + 2] = 0.5 * ((u[1, j, r + t + 2] + mid[1, j, r + t + 2]) + k2)

        return carry

    lax.fori_loop(0, STEPS, step, 0)

    def unpack(r, carry):
        for j in range(blocks):
            for c in range(2):
                buf_f[c, j, pl.ds(r, 8, stride=deep), :] = u[c, j, r + 2]
        return carry

    lax.fori_loop(0, deep, unpack, 0)
    order = spread_order((wide, cols), blocks, 0)
    for c in range(2):
        spread = jnp.concatenate([buf_f[c, j, pl.ds(HALO, rows), :] for j in range(blocks)], axis=1)
        out[c] = shuffle(spread, order)


def propagate(field, levels, halo, table):
    _, rows, cols = field.shape
    tall = rows + 2 * HALO
    blocks = cols // LANES + 1
    wide = blocks * LANES
    deep = tall // 8
    vmem = pl.BlockSpec(memory_space=pltpu.VMEM)
    state = pltpu.VMEM((2, blocks, deep + 4, 8, LANES), F32)
    factor = pltpu.VMEM((blocks, deep, 8, LANES), F32)
    return pl.pallas_call(
        functools.partial(heun_kernel, lax.axis_size("gx")),
        out_shape=jax.ShapeDtypeStruct((2, rows, cols), F32),
        in_specs=[vmem] * 2 + [pl.BlockSpec(memory_space=pltpu.MemorySpace.HBM)] * 4 + [vmem],
        out_specs=vmem,
        scratch_shapes=[
            pltpu.VMEM((2, 2, HALO, wide), F32),
            pltpu.VMEM((2, HALO, wide), jnp.int32),
            pltpu.VMEM((2, rows, LANES), F32),
            pltpu.VMEM((rows, LANES), jnp.int32),
            pltpu.SemaphoreType.DMA((4,)),
            pltpu.VMEM((2, blocks, tall, LANES), F32),
            pltpu.VMEM((blocks, tall, LANES), jnp.int32),
            state,
            state,
            factor,
            factor,
        ],
        compiler_params=pltpu.CompilerParams(vmem_limit_bytes=62 * 1024 * 1024),
        name="heun",
    )(field, levels, *halo, table.reshape(2, LANES))


def split(x):
    big = x.astype(BF16)
    return (big, (x - big.astype(F32)).astype(BF16))


def dot3(a, b):
    dot = functools.partial(jnp.dot, preferred_element_type=F32)
    return dot(a[0], b[0]) + (dot(a[0], b[1]) + dot(a[1], b[0]))


def far_kernel(
    near, e1c, e1s, e2c, e2s, yac, yas, ybc, ybs, out,
    raw, xc, xs, rhs, yc, ys, acc, from_up, from_dn, band, far, give, take,
    raw_send, raw_recv, up_send, up_recv, dn_send, dn_recv, side_send, side_recv,
):
    chunks, _, rows, _ = raw.shape
    groups = acc.shape[1]
    p_rows = acc.shape[2]
    half_q = yc.shape[3]
    ix = lax.axis_index("gx")
    iy = lax.axis_index("gy")
    z = ix // 2
    odd = lax.rem(ix, 2)
    count_x = 2 * groups
    pair = place(ix + 1 - 2 * odd, iy)
    higher = place(lax.rem(ix + 2, count_x), iy)
    lower = place(lax.rem(ix + count_x - 2, count_x), iy)
    side = place(ix, 1 - iy)
    greet([pair, higher, lower, side])

    def remote(src, dst, s, r, device):
        return pltpu.make_async_remote_copy(src, dst, s, r, device_id=device, device_id_type=MESH)

    raws = [
        remote(near.at[:, :, pl.ds(c * LANES, LANES)], raw.at[c], raw_send.at[c], raw_recv.at[c], pair)
        for c in range(chunks)
    ]
    for copy in raws:
        copy.start()

    for o in range(groups):
        a_c, a_s = (e1c[o : o + 1, :], e1s[o : o + 1, :])
        for k, part in enumerate(split(a_c * e2c[...] - a_s * e2s[...])):
            xc[k, pl.ds(o * p_rows, p_rows), :] = part
        for k, part in enumerate(split(a_s * e2c[...] + a_c * e2s[...])):
            xs[k, pl.ds(o * p_rows, p_rows), :] = part
    fine = ybc.shape[0]
    for h in range(2):
        q = pl.ds(h * half_q, half_q)
        for o in range(yac.shape[0]):
            a_c, a_s = (yac[o : o + 1, q], yas[o : o + 1, q])
            y = pl.ds(o * fine, fine)
            for k, part in enumerate(split(a_c * ybc[:, q] - a_s * ybs[:, q])):
                yc[h, k, y, :] = part
            for k, part in enumerate(split(a_s * ybc[:, q] + a_c * ybs[:, q])):
                ys[h, k, y, :] = part

    def up_copy(c, o):
        return remote(acc.at[c, o], from_up.at[c, o], up_send.at[c, o], up_recv.at[c, o], higher)

    def dn_copy(c, o):
        return remote(acc.at[c, o], from_dn.at[c, o], dn_send.at[c, o], dn_recv.at[c, o], lower)

    def transform(c):
        raws[c].wait_recv()
        mine = pl.ds(pl.multiple_of(odd * rows, rows), rows)
        theirs = pl.ds(pl.multiple_of((1 - odd) * rows, rows), rows)
        for d in range(2):
            lanes = pl.ds(d * LANES, LANES)
            for k, part in enumerate(split(near[d, :, pl.ds(c * LANES, LANES)])):
                rhs[k, mine, lanes] = part
            for k, part in enumerate(split(raw[c, d])):
                rhs[k, theirs, lanes] = part
        right = (rhs[0], rhs[1])
        by_cos = dot3((xc[0], xc[1]), right)
        by_sin = dot3((xs[0], xs[1]), right)
        re = by_cos[:, :LANES] + by_sin[:, LANES:]
        im = by_cos[:, LANES:] - by_sin[:, :LANES]
        for o in range(groups):
            acc[c, o, :, pl.ds(0, LANES)] = re[o * p_rows : (o + 1) * p_rows]
            acc[c, o, :, pl.ds(LANES, LANES)] = im[o * p_rows : (o + 1) * p_rows]

    def originate(c):
        @pl.when(z == 0)
        def _():
            for o in reversed(range(1, groups)):
                up_copy(c, o).start()

        @pl.when(z == groups - 1)
        def _():
            for o in range(groups - 1):
                dn_copy(c, o).start()

    def forward(c):
        for k in range(groups):
            far_up, far_dn = (groups - 1 - k, k)

            @pl.when((z > 0) & (z < far_up))
            def _():
                up_copy(c, far_up).wait_recv()
                acc[c, far_up] += from_up[c, far_up]
                up_copy(c, far_up).start()

            @pl.when((z < groups - 1) & (z > far_dn))
            def _():
                dn_copy(c, far_dn).wait_recv()
                acc[c, far_dn] += from_dn[c, far_dn]
                dn_copy(c, far_dn).start()

    def collect(g):
        for o in range(groups):

            @pl.when(z == o)
            def _():
                for i in range(2):
                    c = 2 * g + i
                    total = acc[c, o]
                    if o > 0:
                        up_copy(c, o).wait_recv()
                        total = total + from_up[c, o]
                    if o < groups - 1:
                        dn_copy(c, o).wait_recv()
                        total = total + from_dn[c, o]
                    for k, part in enumerate(split(total)):
                        band[g, k, pl.ds(0, p_rows), pl.ds(i * LANES, LANES)] = part[:, :LANES]
                        band[g, k, pl.ds(p_rows, p_rows), pl.ds(i * LANES, LANES)] = part[:, LANES:]

    def angles(g, h):
        left = (band[g, 0], band[g, 1])
        y = pl.ds(2 * g * LANES, 2 * LANES)
        by_cos = dot3(left, (yc[h, 0, y], yc[h, 1, y]))
        by_sin = dot3(left, (ys[h, 0, y], ys[h, 1, y]))
        return (by_cos[:p_rows] + by_sin[p_rows:], by_cos[p_rows:] - by_sin[:p_rows])

    final = chunks // 2 - 1

    def accumulate(g):
        for h in range(2):
            for d, value in enumerate(angles(g, h)):
                far[h, d] = value if g == 0 else far[h, d] + value

    for c in range(chunks):
        transform(c)
        originate(c)
        if c > 0:
            forward(c - 1)
        if c >= 3 and c % 2 == 1:
            collect(c // 2 - 1)
            accumulate(c // 2 - 1)
    forward(chunks - 1)
    collect(final)

    def finish(h):
        pair_of = angles(final, h)
        return [far[h, d] + pair_of[d] for d in range(2)]

    give[0], give[1] = finish(1 - iy)
    swap = remote(give, take, side_send.at[0], side_recv.at[0], side)
    swap.start()
    re, im = finish(iy)
    swap.wait_recv()
    out[0] = re + take[0]
    out[1] = im + take[1]

    swap.wait_send()
    for copy in raws:
        copy.wait_send()
    for c in range(chunks):
        for o in range(groups):

            @pl.when(z < o)
            def _():
                up_copy(c, o).wait_send()

            @pl.when(z > o)
            def _():
                dn_copy(c, o).wait_send()


def turn(phase, total, scale):
    angle = 2.0 * math.pi / total * (phase % total).astype(F32)
    return (jnp.cos(angle) * scale, jnp.sin(angle) * scale)


def tables(rows, cols, count_x, count_y):
    index_x = lax.axis_index("gx")
    index_y = lax.axis_index("gy")
    total_x = rows * count_x
    total_y = cols * count_y
    p_rows = P_SIZE // count_x
    x = (index_x // 2) * 2 * rows + jnp.arange(2 * rows, dtype=jnp.int32)
    first = (2 * jnp.arange(count_x // 2, dtype=jnp.int32) + index_x % 2) * p_rows
    base = first + total_x - P_SIZE // 2
    e1 = turn(base[:, None] * x[None, :], total_x, 1.0 / math.sqrt(total_x))
    e2 = turn(jnp.arange(p_rows, dtype=jnp.int32)[:, None] * x[None, :], total_x, 1.0)
    fine = 32
    q = jnp.arange(Q, dtype=jnp.int32) + total_y - Q // 2
    coarse = index_y * cols + fine * jnp.arange(cols // fine, dtype=jnp.int32)
    ya = turn(coarse[:, None] * q[None, :], total_y, 1.0 / math.sqrt(total_y))
    yb = turn(jnp.arange(fine, dtype=jnp.int32)[:, None] * q[None, :], total_y, 1.0)
    return (*e1, *e2, *ya, *yb)


def far(near, angles, count_x):
    _, rows, cols = near.shape
    groups = count_x // 2
    p_rows = P_SIZE // count_x
    chunks = cols // LANES
    half_q = Q // 2
    vmem = pl.BlockSpec(memory_space=pltpu.VMEM)
    dma = pltpu.SemaphoreType.DMA
    stage = pltpu.VMEM((chunks, groups, p_rows, 2 * LANES), F32)
    return pl.pallas_call(
        far_kernel,
        out_shape=jax.ShapeDtypeStruct((2, p_rows, half_q), F32),
        in_specs=[vmem] * 9,
        out_specs=vmem,
        scratch_shapes=[
            pltpu.VMEM((chunks, 2, rows, LANES), F32),
            pltpu.VMEM((2, groups * p_rows, 2 * rows), BF16),
            pltpu.VMEM((2, groups * p_rows, 2 * rows), BF16),
            pltpu.VMEM((2, 2 * rows, 2 * LANES), BF16),
            pltpu.VMEM((2, 2, cols, half_q), BF16),
            pltpu.VMEM((2, 2, cols, half_q), BF16),
            stage,
            stage,
            stage,
            pltpu.VMEM((chunks // 2, 2, 2 * p_rows, 2 * LANES), BF16),
            pltpu.VMEM((2, 2, p_rows, half_q), F32),
            pltpu.VMEM((2, p_rows, half_q), F32),
            pltpu.VMEM((2, p_rows, half_q), F32),
            dma((chunks,)),
            dma((chunks,)),
            dma((chunks, groups)),
            dma((chunks, groups)),
            dma((chunks, groups)),
            dma((chunks, groups)),
            dma((1,)),
            dma((1,)),
        ],
        compiler_params=pltpu.CompilerParams(
            collective_id=1, has_side_effects=True, vmem_limit_bytes=48 * 1024 * 1024
        ),
        name="far",
    )(near, *angles)


def on_device(field, levels, table):
    _, rows, cols = field.shape
    count_x = lax.axis_size("gx")
    angles = tables(rows, cols, count_x, lax.axis_size("gy"))
    near = propagate(field, levels, gather_halo(field, levels), table)
    return (near, jnp.transpose(far(near, angles, count_x), (1, 0, 2)))


def solution(mesh):
    in_specs = (P(None, ("parts", "gx"), "gy"), P(("parts", "gx"), "gy"), P())
    out_specs = (P(None, ("parts", "gx"), "gy"), P(("parts", "gx"), None, "gy"))
    return jax.shard_map(
        on_device, mesh=mesh, in_specs=in_specs, out_specs=out_specs, check_vma=False
    )
```
